512 devices in a mesh: lat: 8 (over z_hi, core), lon: 64 (over z_lo, y, x).
Axes of the slice: x: 4, y: 8, z: 8 (z_hi: 4, z_lo: 2; z = z_hi * 2 + z_lo), core: 2. Of those that a mesh axis runs over, the one named last changes fastest.
Arguments:
- field: bfloat16 [64, 1024, 256], P('lat', 'lon'), may hold values from -6 to 6
- dw_weight: bfloat16 [7, 7, 256], replicated, may hold values from -0.875 to 0.875
- w_expand: bfloat16 [256, 1024], replicated, may hold values from -0.375 to 0.375
- w_reduce: bfloat16 [1024, 256], replicated, may hold values from -0.1875 to 0.1875
- lat_attn: bfloat16 [4, 256, 256], replicated, as said below
- lon_attn: bfloat16 [4, 256, 256], replicated, as said below
Outputs:
- result: bfloat16 [64, 1024, 256], P('lat', 'lon')
The draws below stay inside these ranges and needn't reach their ends.
Inputs may be any that keep to these rules, and one draw needn't show every extreme that they name: `lat_attn`: query, key, value and output projections in this order. `lon_attn`: query, key, value and output projections in this order.
All inputs are finite; a program needn't handle non-finite values.
Results may differ from the reference program's by a relative error of at most 0.03.
Values may be sent and summed in bfloat16 or wider, within the bound.
A program may use at most 64 MiB of HBM per device.

```python
import jax
import jax.numpy as jnp
from jax import lax

C = 256
HEADS = 8
HID = 1024
NLAT = 64
NLON = 1024


def attention_weights(key, marker):
    base = jax.random.fold_in(key, marker)
    entries = jax.random.normal(base, (4, C, C), jnp.float32) * C ** (-0.5)
    return entries.astype(jnp.bfloat16)


def draw_lat_attn(key, part):
    return attention_weights(key, 11)


def draw_lon_attn(key, part):
    return attention_weights(key, 23)


def level_of(stream_key, dims, split, low, largest):
    loudness = 1.0
    for position, blocks in split:
        draws = jax.random.uniform(jax.random.fold_in(jax.random.fold_in(stream_key, 6), position), (blocks,), jnp.float32, low / len(split), largest / len(split))
        loudness = loudness * jnp.repeat(jnp.exp(draws), dims[position] // blocks).reshape((-1,) + (1,) * (len(dims) - 1 - position))
    return loudness


def normal_values(key, extent, spread, bound, shards=(), kind=jnp.bfloat16):
    values = spread * jax.random.normal(key, extent, jnp.float32)
    if shards:
        values = values * level_of(key, extent, shards, -0.22, 0.18)
    return jnp.clip(values, -bound, bound).astype(kind)


def setup_inputs(seed: int = 0) -> dict:
    keys = jax.random.split(jax.random.key(seed), 7)
    return {
        "field": normal_values(keys[0], (NLAT, NLON, C), 1.0, 6.0, ((0, 8), (1, 64))),
        "dw_weight": normal_values(keys[1], (7, 7, C), 49 ** -0.5, 0.875),
        "w_expand": normal_values(keys[2], (C, HID), C ** -0.5, 0.375),
        "w_reduce": normal_values(keys[3], (HID, C), HID ** -0.5, 0.1875),
        "lat_attn": draw_lat_attn(jax.random.fold_in(keys[6], 71), 0),
        "lon_attn": draw_lon_attn(jax.random.fold_in(keys[6], 71), 0),
    }


EPSILON = 1e-06

def layer_norm(values):
    average = lax.optimization_barrier(jnp.mean(values, axis=-1, keepdims=True))
    centered = values - average
    variance = lax.optimization_barrier(jnp.mean(centered * centered, axis=-1, keepdims=True))
    return centered * lax.rsqrt(variance + EPSILON)

def project(rows, matrix):
    shape = rows.shape
    flat_rows = rows.reshape(-1, shape[-1])
    product = jnp.dot(flat_rows, matrix, preferred_element_type=jnp.float32)
    return product.reshape(shape[:-1] + (matrix.shape[1],))

def row_attention(sequence, weights):
    count, length, channels = sequence.shape
    head_size = channels // HEADS
    queries = project(sequence, weights[0]).astype(jnp.bfloat16).reshape(count, length, HEADS, head_size)
    key_all = project(sequence, weights[1]).astype(jnp.bfloat16).reshape(count, length, HEADS, head_size)
    value_all = project(sequence, weights[2]).astype(jnp.bfloat16).reshape(count, length, HEADS, head_size)

    def single_row(operands):
        query_row, key_row, value_row = operands
        scores = jnp.einsum('qhd,khd->hqk', query_row.astype(jnp.float32), key_row.astype(jnp.float32), precision=lax.Precision.HIGHEST) * head_size ** (-0.5)
        top = lax.optimization_barrier(jnp.max(scores, axis=-1, keepdims=True))
        raw_weights = jnp.exp(scores - top)
        totals = lax.optimization_barrier(jnp.sum(raw_weights, axis=-1))
        rounded = lax.optimization_barrier(raw_weights.astype(jnp.bfloat16)).astype(jnp.float32)
        mixed = jnp.einsum('hqk,khd->hqd', rounded, value_row.astype(jnp.float32), precision=lax.Precision.HIGHEST)
        mixed = mixed / totals[..., None]
        return jnp.swapaxes(mixed, 0, 1).reshape(length, channels).astype(jnp.bfloat16)
    return lax.map(single_row, (queries, key_all, value_all))

def reference(field, dw_weight, w_expand, w_reduce, lat_attn, lon_attn):
    field_wide = field.astype(jnp.float32)
    padded = jnp.pad(field_wide, ((3, 3), (0, 0), (0, 0)))
    padded = jnp.concatenate([padded[:, -3:], padded, padded[:, :3]], axis=1)
    taps = dw_weight.astype(jnp.float32)
    convolved = jnp.zeros_like(field_wide)
    for row_off in range(7):
        for col_off in range(7):
            convolved = convolved + padded[row_off:row_off + NLAT, col_off:col_off + NLON] * taps[row_off, col_off]
    normed = layer_norm(convolved).astype(jnp.bfloat16)
    expanded = jax.nn.gelu(project(normed, w_expand), approximate=False).astype(jnp.bfloat16)
    block_one = (field_wide + project(expanded, w_reduce)).astype(jnp.bfloat16)
    lat_in = layer_norm(block_one.astype(jnp.float32)).astype(jnp.bfloat16)
    lat_mix = jnp.swapaxes(row_attention(jnp.swapaxes(lat_in, 0, 1), lat_attn), 0, 1)
    block_two = (block_one.astype(jnp.float32) + project(lat_mix, lat_attn[3])).astype(jnp.bfloat16)
    lon_in = layer_norm(block_two.astype(jnp.float32)).astype(jnp.bfloat16)
    lon_mix = row_attention(lon_in, lon_attn)
    return (block_two.astype(jnp.float32) + project(lon_mix, lon_attn[3])).astype(jnp.bfloat16)
```

```python
import jax
import jax.numpy as jnp
from jax import lax
from jax.sharding import PartitionSpec as P

HEADS = 8


EPSILON = 1e-06


def padded_2(array, sides, width, wrap):
    for axis, dim in sides:
        devices, length = (lax.axis_size(axis), array.shape[dim])
        up = [(i, (i + 1) % devices) for i in range(devices if wrap else devices - 1)]
        down = [(j, i) for i, j in up]
        last = lax.slice_in_dim(array, length - width, length, axis=dim)
        first = lax.slice_in_dim(array, 0, width, axis=dim)
        before = lax.ppermute(last, axis, up)
        after = lax.ppermute(first, axis, down)
        array = jnp.concatenate([before, array, after], axis=dim)
    return array


def layer_norm(values):
    average = jnp.mean(values, axis=-1, keepdims=True)
    centered = values - average
    variance = jnp.mean(centered * centered, axis=-1, keepdims=True)
    return centered * lax.rsqrt(variance + EPSILON)


def project(rows, matrix):
    shape = rows.shape
    flat_rows = rows.reshape(-1, shape[-1])
    product = jnp.dot(flat_rows, matrix, preferred_element_type=jnp.float32)
    return product.reshape(shape[:-1] + (matrix.shape[1],))


def row_attention(sequence, weights):
    count, length, channels = sequence.shape
    head_size = channels // HEADS
    queries = (
        project(sequence, weights[0]).astype(jnp.bfloat16).reshape(count, length, HEADS, head_size)
    )
    key_all = (
        project(sequence, weights[1]).astype(jnp.bfloat16).reshape(count, length, HEADS, head_size)
    )
    value_all = (
        project(sequence, weights[2]).astype(jnp.bfloat16).reshape(count, length, HEADS, head_size)
    )
    scores = jnp.einsum(
        "rqhd,rkhd->rhqk", queries, key_all, preferred_element_type=jnp.float32
    ) * head_size ** (-0.5)
    top = jnp.max(scores, axis=-1, keepdims=True)
    raw_weights = jnp.exp(scores - top)
    totals = jnp.sum(raw_weights, axis=-1)
    mixed = jnp.einsum(
        "rhqk,rkhd->rqhd",
        raw_weights.astype(jnp.bfloat16),
        value_all,
        preferred_element_type=jnp.float32,
    )
    mixed = mixed / jnp.swapaxes(totals, 1, 2)[..., None]
    return mixed.reshape(count, length, channels).astype(jnp.bfloat16)


def shards(field, dw_weight, w_expand, w_reduce, lat_attn, lon_attn):
    lat_rows, lon_cols, channels = field.shape
    head_size = channels // HEADS
    score_scale = head_size ** (-0.5)
    lat_groups = lax.axis_size("lat")
    padded = padded_2(field, (("lat", 0),), 3, False)
    padded = padded_2(padded, (("lon", 1),), 3, True).astype(jnp.float32)
    taps = dw_weight.astype(jnp.float32)
    field_wide = field.astype(jnp.float32)
    convolved = jnp.zeros_like(field_wide)
    for row_off in range(7):
        for col_off in range(7):
            convolved = (
                convolved
                + padded[row_off : row_off + lat_rows, col_off : col_off + lon_cols]
                * taps[row_off, col_off]
            )
    normed = layer_norm(convolved).astype(jnp.bfloat16)
    expanded = jax.nn.gelu(project(normed, w_expand), approximate=False).astype(jnp.bfloat16)
    block_one = (field_wide + project(expanded, w_reduce)).astype(jnp.bfloat16)
    lat_in = layer_norm(block_one.astype(jnp.float32)).astype(jnp.bfloat16)
    grouped = lat_in.reshape(lat_rows, lat_groups, lon_cols // lat_groups, channels)
    flat_columns = lax.all_to_all(grouped, "lat", split_axis=1, concat_axis=0, tiled=True)[:, 0]
    mixed_columns = jnp.swapaxes(row_attention(jnp.swapaxes(flat_columns, 0, 1), lat_attn), 0, 1)
    lat_mix = mixed_columns[:, None]
    lat_back = lax.all_to_all(lat_mix, "lat", split_axis=0, concat_axis=1, tiled=True).reshape(
        lat_rows, lon_cols, channels
    )
    block_two = (block_one.astype(jnp.float32) + project(lat_back, lat_attn[3])).astype(
        jnp.bfloat16
    )
    lon_in = layer_norm(block_two.astype(jnp.float32)).astype(jnp.bfloat16)
    weights = jnp.transpose(lon_attn[:3].reshape(3, channels, HEADS, head_size), (1, 2, 0, 3))
    packed = project(lon_in, weights.reshape(channels, -1)).astype(jnp.bfloat16)
    packed = packed.reshape(lat_rows, lon_cols, HEADS, 3 * head_size)
    packed = packed.transpose(0, 2, 1, 3).reshape(lat_rows * HEADS, lon_cols, 3 * head_size)
    row = lax.all_to_all(packed, "lon", split_axis=0, concat_axis=0, tiled=True)
    row = row.reshape(-1, 3, head_size)
    scores = jnp.dot(row[:, 0], row[:, 1].T, preferred_element_type=jnp.float32) * score_scale
    probs = jnp.exp(scores - jnp.max(scores, axis=-1, keepdims=True))
    totals = jnp.sum(probs, axis=-1, keepdims=True)
    mixed = jnp.dot(probs.astype(jnp.bfloat16), row[:, 2], preferred_element_type=jnp.float32)
    mixed = (mixed / totals).astype(jnp.bfloat16).reshape(-1, lon_cols, head_size)
    back = lax.all_to_all(mixed, "lon", split_axis=0, concat_axis=0, tiled=True)
    back = back.reshape(lat_rows, HEADS, lon_cols, head_size)
    mixture = back.transpose(0, 2, 1, 3).reshape(lat_rows, lon_cols, channels)
    return (block_two.astype(jnp.float32) + project(mixture, lon_attn[3])).astype(jnp.bfloat16)


def solution(mesh):
    return jax.shard_map(
        shards,
        mesh=mesh,
        in_specs=(P("lat", "lon", None), P(), P(), P(), P(), P()),
        out_specs=P("lat", "lon", None),
        check_vma=False,
    )
```

```python
import functools
import math

import jax
import jax.numpy as jnp
from jax import lax
from jax.experimental import pallas as pl
from jax.experimental.pallas import tpu as pltpu
from jax.sharding import PartitionSpec as P

HEADS = 8
EPSILON = 1e-06
REACH = 3
TILE = 128
MESH = pl.DeviceIdType.MESH


def layer_norm(values):
    average = jnp.mean(values, axis=-1, keepdims=True)
    centered = values - average
    variance = jnp.mean(centered * centered, axis=-1, keepdims=True)
    return centered * lax.rsqrt(variance + EPSILON)


def dot(left, right):
    return jnp.dot(left, right, preferred_element_type=jnp.float32)


def dot_t(left, right):
    return lax.dot_general(left, right, (((1,), (1,)), ((), ())), preferred_element_type=jnp.float32)


def iotas(shape):
    return (lax.broadcasted_iota(jnp.int32, shape, 0), lax.broadcasted_iota(jnp.int32, shape, 1))


def wide(ref):
    return ref[...].astype(jnp.float32)


def kernel(
    lats,
    lons,
    field_hbm,
    taps_hbm,
    expand_hbm,
    reduce_hbm,
    lat_attn_hbm,
    lon_attn_hbm,
    out_ref,
    field,
    taps,
    expand,
    reduce,
    lat_attn,
    lon_attn,
    edge_first,
    edge_last,
    top,
    bottom,
    left,
    right,
    padded,
    taps_wide,
    convolved,
    packed_weights,
    lat_out,
    lat_rows,
    lat_mix_out,
    lat_mix_rows,
    lon_out,
    lon_rows,
    lon_mix_out,
    lon_mix_rows,
    load_sems,
    halo_send,
    halo_recv,
    group_send,
    group_recv,
):
    rows, cols, channels = field.shape
    cells = rows * cols
    head_size = channels // HEADS
    per_tile = TILE // head_size
    lat, lon = lax.axis_index("lat"), lax.axis_index("lon")

    loads = [
        pltpu.make_async_copy(source, target, load_sems.at[index])
        for index, (source, target) in enumerate(
            (
                (field_hbm, field),
                (taps_hbm, taps),
                (lon_attn_hbm, lon_attn),
                (expand_hbm, expand),
                (reduce_hbm, reduce),
                (lat_attn_hbm, lat_attn),
            )
        )
    ]
    for load in loads:
        load.start()

    north, south = lax.rem(lat + lats - 1, lats), lax.rem(lat + 1, lats)
    west, east = lax.rem(lon + lons - 1, lons), lax.rem(lon + 1, lons)

    barrier = pltpu.get_barrier_semaphore()

    def greet(place):
        pl.semaphore_signal(barrier, inc=1, device_id=place, device_id_type=MESH)

    for place in ((north, west), (north, east), (south, west), (south, east)):
        greet(place)

    def greet_lat(step, carry):
        greet((lax.rem(lat + step, lats), lon))
        return carry

    def greet_lon(step, carry):
        greet((lat, lax.rem(lon + step, lons)))
        return carry

    lax.fori_loop(1, lats, greet_lat, 0)
    lax.fori_loop(1, lons, greet_lon, 0)

    loads[0].wait()
    edge_first[...] = field[:, :4]
    edge_last[...] = field[:, cols - 4 :]
    pl.semaphore_wait(barrier, 4 + lats - 1 + lons - 1)

    tail, head = pl.ds(rows - REACH, REACH), pl.ds(0, REACH)
    after, inner = pl.ds(rows + REACH, REACH), pl.ds(REACH, rows)
    halos = []
    for index, (source, target, place) in enumerate(
        (
            (edge_last, left.at[inner], (lat, east)),
            (edge_first, right.at[inner], (lat, west)),
            (field.at[tail], top, (south, lon)),
            (field.at[head], bottom, (north, lon)),
            (edge_last.at[tail], left.at[head], (south, east)),
            (edge_last.at[head], left.at[after], (north, east)),
            (edge_first.at[tail], right.at[head], (south, west)),
            (edge_first.at[head], right.at[after], (north, west)),
        )
    ):
        copy = pltpu.make_async_remote_copy(
            src_ref=source,
            dst_ref=target,
            send_sem=halo_send.at[index],
            recv_sem=halo_recv.at[index],
            device_id=place,
            device_id_type=MESH,
        )
        copy.start()
        halos.append(copy)

    def exchange(phase, source_of, target):
        axis_lat = phase < 2
        members, me = (lats, lat) if axis_lat else (lons, lon)

        def copy_to(source, slot, place):
            return pltpu.make_async_remote_copy(
                src_ref=source,
                dst_ref=slot,
                send_sem=group_send.at[phase],
                recv_sem=group_recv.at[phase],
                device_id=place,
                device_id_type=MESH,
            )

        def send(step, carry):
            other = lax.rem(me + step, members)
            place = (other, lon) if axis_lat else (lat, other)
            copy_to(source_of(other), target.at[me], place).start()
            return carry

        lax.fori_loop(1, members, send, 0)
        target[me] = source_of(me)[...]
        others = target.at[pl.ds(0, members - 1)]
        return copy_to(others, others, (lat, lon))

    loads[1].wait()
    taps_wide[...] = taps[...].astype(jnp.float32)
    padded[pl.ds(REACH, rows), 8 : 8 + cols] = wide(field)

    loads[2].wait()
    lane = lax.broadcasted_iota(jnp.int32, (channels, TILE), 1)
    for head_index in range(HEADS):
        tile = pl.ds(head_index // per_tile * TILE, TILE)
        shift = head_index % per_tile * head_size
        parts = [
            pltpu.roll(
                lon_attn[kind, :, tile].astype(jnp.float32), (kind * head_size - shift) % TILE, 1
            )
            for kind in range(3)
        ]
        block = jnp.where(
            lane < head_size,
            parts[0],
            jnp.where(
                lane < 2 * head_size, parts[1], jnp.where(lane < 3 * head_size, parts[2], 0.0)
            ),
        )
        packed_weights[:, head_index * TILE : (head_index + 1) * TILE] = block.astype(jnp.bfloat16)
    loads[3].wait()
    loads[4].wait()
    loads[5].wait()

    for copy in halos:
        copy.wait_recv()
    not_first = (lat > 0).astype(jnp.float32)
    not_last = (lat < lats - 1).astype(jnp.float32)
    padded[pl.ds(0, REACH), 8 : 8 + cols] = wide(top) * not_first
    padded[pl.ds(rows + REACH, REACH), 8 : 8 + cols] = wide(bottom) * not_last
    for side, start in ((left, 4), (right, 8 + cols)):
        values = wide(side)
        padded[pl.ds(0, REACH), start : start + 4] = values[:REACH] * not_first
        padded[pl.ds(REACH, rows), start : start + 4] = values[REACH : REACH + rows]
        padded[pl.ds(rows + REACH, REACH), start : start + 4] = values[REACH + rows :] * not_last

    for half in range(channels // TILE):
        lanes = pl.ds(half * TILE, TILE)
        total = jnp.zeros((rows, cols, TILE), jnp.float32)
        for col_off in range(2 * REACH + 1):
            view = padded[:, 8 - REACH + col_off : 8 - REACH + col_off + cols, lanes]
            for row_off in range(2 * REACH + 1):
                tap = taps_wide[row_off, col_off : col_off + 1, lanes]
                total = total + view[row_off : row_off + rows] * tap
        convolved[:, lanes] = total.reshape(cells, TILE)

    normed = layer_norm(convolved[...]).astype(jnp.bfloat16)
    hidden = dot(normed, expand[...])
    hidden = 0.5 * hidden * (1.0 + lax.erf(hidden * (0.5**0.5)))
    own = field[...].astype(jnp.float32).reshape(cells, channels)
    block_one = (own + dot(hidden.astype(jnp.bfloat16), reduce[...])).astype(jnp.bfloat16)
    lat_in = layer_norm(block_one.astype(jnp.float32)).astype(jnp.bfloat16)

    into, out_of = iotas((cells, cells))
    to_lon = (into // rows == out_of % cols) & (into % rows == out_of // cols)
    to_lat = (into % cols == out_of // rows) & (into // cols == out_of % rows)
    to_lon = to_lon.astype(jnp.float32).astype(jnp.bfloat16)
    to_lat = to_lat.astype(jnp.float32).astype(jnp.bfloat16)
    by_lon = dot(to_lon, lat_in).astype(jnp.bfloat16)
    block_rows = cells // lats
    lat_out[...] = by_lon.reshape(lats, block_rows, channels)
    pending = exchange(0, lambda member: lat_out.at[member], lat_rows)
    pending.wait_recv()

    column = lat_rows[...].reshape(cells, channels)
    scale = head_size ** (-0.5) * math.log2(math.e)
    queries = (dot(column, lat_attn[0]) * scale).astype(jnp.bfloat16)
    keys = dot(column, lat_attn[1]).astype(jnp.bfloat16)
    values = dot(column, lat_attn[2]).astype(jnp.bfloat16)
    lane = lax.broadcasted_iota(jnp.int32, (cells, channels), 1)
    query_row, key_row = iotas((cells, cells))
    same = query_row // rows % (block_rows // rows) == key_row // rows % (block_rows // rows)
    mixed = jnp.zeros((cells, channels), jnp.float32)
    for head_index in range(HEADS):
        mine = lane // head_size == head_index
        scores = dot_t(queries, jnp.where(mine, keys, jnp.zeros_like(keys)))
        scores = jnp.where(same, scores, -1e30)
        probs = jnp.exp2(scores - jnp.max(scores, axis=-1, keepdims=True))
        probs = probs / jnp.sum(probs, axis=-1, keepdims=True)
        mixed = mixed + dot(
            probs.astype(jnp.bfloat16), jnp.where(mine, values, jnp.zeros_like(values))
        )
    lat_mix_out[...] = mixed.astype(jnp.bfloat16).reshape(lats, block_rows, channels)
    pending.wait_send()
    pending = exchange(1, lambda member: lat_mix_out.at[member], lat_mix_rows)
    pending.wait_recv()

    lat_mix = dot(to_lat, lat_mix_rows[...].reshape(cells, channels)).astype(jnp.bfloat16)
    block_two = block_one.astype(jnp.float32) + dot(lat_mix, lat_attn[3])
    block_two = block_two.astype(jnp.bfloat16)
    lon_in = layer_norm(block_two.astype(jnp.float32)).astype(jnp.bfloat16)
    lane = lax.broadcasted_iota(jnp.int32, (cells, TILE), 1)
    scales = jnp.where(lane < head_size, scale, 1.0)
    for head_index in range(HEADS):
        block = dot(lon_in, packed_weights[:, head_index * TILE : (head_index + 1) * TILE])
        lon_out[:, head_index] = (block * scales).astype(jnp.bfloat16).reshape(rows, cols, TILE)
    pending.wait_send()
    pending = exchange(
        2, lambda member: lon_out.at[member // HEADS, lax.rem(member, HEADS)], lon_rows
    )
    pending.wait_recv()

    length = lons * cols
    row = lon_rows[...].reshape(length, TILE)
    place = lax.rem(lon, per_tile) * head_size
    source, target = iotas((TILE, 2 * TILE))
    key_spot = (target < head_size) & (source == target + head_size)
    value_spot = (
        (target >= TILE + place)
        & (target < TILE + place + head_size)
        & (source == target - TILE - place + 2 * head_size)
    )
    select = (key_spot | value_spot).astype(jnp.float32).astype(jnp.bfloat16)
    moved = dot(row, select).astype(jnp.bfloat16)
    keys = moved[:, :TILE]
    values = jnp.concatenate([moved[:, TILE:], jnp.ones((length, TILE), jnp.bfloat16)], axis=1)
    lane = lax.broadcasted_iota(jnp.int32, (length, TILE), 1)
    queries = jnp.where(lane < head_size, row, jnp.zeros_like(row))
    chunk = 256
    for start in range(0, length, chunk):
        scores = dot_t(queries[start : start + chunk], keys)
        probs = jnp.exp2(scores - jnp.max(scores, axis=-1, keepdims=True))
        mixed = dot(probs.astype(jnp.bfloat16), values)
        mixed = (mixed[:, :TILE] / mixed[:, TILE:]).astype(jnp.bfloat16)
        lon_mix_out[start // cols : (start + chunk) // cols] = mixed.reshape(
            chunk // cols, cols, TILE
        )
    pending.wait_send()
    pending = exchange(3, lambda member: lon_mix_out.at[member], lon_mix_rows)
    pending.wait_recv()

    result = block_two.astype(jnp.float32)
    for tile in range(channels // TILE):
        total = jnp.zeros((rows, cols, TILE), jnp.float32)
        for head_index in range(per_tile * tile, per_tile * (tile + 1)):
            for_rows = [
                lon_mix_rows[row_index * HEADS + head_index].astype(jnp.float32)
                for row_index in range(rows)
            ]
            total = total + jnp.stack(for_rows)
        mixture = total.reshape(cells, TILE).astype(jnp.bfloat16)
        result = result + dot(mixture, lon_attn[3, tile * TILE : (tile + 1) * TILE])
    out_ref[...] = result.astype(jnp.bfloat16).reshape(rows, cols, channels)
    pending.wait_send()
    for copy in halos:
        copy.wait_send()


def shards(lats, lons, field, dw_weight, w_expand, w_reduce, lat_attn, lon_attn):
    rows, cols, channels = field.shape
    cells = rows * cols
    bf16, f32 = jnp.bfloat16, jnp.float32
    arguments = (field, dw_weight, w_expand, w_reduce, lat_attn, lon_attn)
    vmem = pltpu.VMEM
    edge = vmem((rows, 4, channels), bf16)
    strip = vmem((REACH, cols, channels), bf16)
    side = vmem((rows + 2 * REACH, 4, channels), bf16)
    column = vmem((lats, cells // lats, channels), bf16)
    row = vmem((lons, cols, TILE), bf16)
    return pl.pallas_call(
        functools.partial(kernel, lats, lons),
        out_shape=jax.ShapeDtypeStruct(field.shape, field.dtype),
        in_specs=[pl.BlockSpec(memory_space=pl.ANY)] * len(arguments),
        out_specs=pl.BlockSpec(memory_space=pltpu.VMEM),
        scratch_shapes=[
            *(vmem(argument.shape, argument.dtype) for argument in arguments),
            edge,
            edge,
            strip,
            strip,
            side,
            side,
            vmem((rows + 2 * REACH, cols + 16, channels), f32),
            vmem(dw_weight.shape, f32),
            vmem((cells, channels), f32),
            vmem((channels, HEADS * TILE), bf16),
            column,
            column,
            column,
            column,
            vmem((rows, HEADS, cols, TILE), bf16),
            row,
            row,
            row,
            pltpu.SemaphoreType.DMA((len(arguments),)),
            pltpu.SemaphoreType.DMA((8,)),
            pltpu.SemaphoreType.DMA((8,)),
            pltpu.SemaphoreType.DMA((4,)),
            pltpu.SemaphoreType.DMA((4,)),
        ],
        compiler_params=pltpu.CompilerParams(
            collective_id=0, has_side_effects=True, vmem_limit_bytes=48 << 20
        ),
        name="block",
    )(*arguments)


def solution(mesh):
    return jax.shard_map(
        functools.partial(shards, mesh.shape["lat"], mesh.shape["lon"]),
        mesh=mesh,
        in_specs=(P("lat", "lon", None), P(), P(), P(), P(), P()),
        out_specs=P("lat", "lon", None),
        check_vma=False,
    )
```

```python
import functools
import math

import jax
import jax.numpy as jnp
from jax import lax
from jax.experimental import pallas as pl
from jax.experimental.pallas import tpu as pltpu
from jax.sharding import PartitionSpec as P

HEADS = 8
EPSILON = 1e-06
REACH = 3
TILE = 128
PACK = 4
MESH = pl.DeviceIdType.MESH


def layer_norm(values):
    average = jnp.mean(values, axis=-1, keepdims=True)
    centered = values - average
    variance = jnp.mean(centered * centered, axis=-1, keepdims=True)
    return centered * lax.rsqrt(variance + EPSILON)


def dot(left, right):
    return jnp.dot(left, right, preferred_element_type=jnp.float32)


def dot_t(left, right):
    return lax.dot_general(left, right, (((1,), (1,)), ((), ())), preferred_element_type=jnp.float32)


def iotas(shape):
    return (lax.broadcasted_iota(jnp.int32, shape, 0), lax.broadcasted_iota(jnp.int32, shape, 1))


def wide(ref):
    return ref[...].astype(jnp.float32)


def kernel(
    lats,
    lons,
    field_hbm,
    taps_hbm,
    expand_hbm,
    reduce_hbm,
    lat_attn_hbm,
    lon_attn_hbm,
    out_ref,
    field,
    taps,
    expand,
    reduce,
    lat_attn,
    lon_attn,
    edge_first,
    edge_last,
    top,
    bottom,
    left,
    right,
    padded,
    taps_wide,
    convolved,
    orders,
    block_packed,
    lat_out,
    lat_rows,
    lat_mix_out,
    lat_mix_rows,
    lon_out,
    lon_rows,
    lon_mix_out,
    lon_mix_rows,
    load_sems,
    halo_send,
    halo_recv,
    group_send,
    group_recv,
):
    rows, cols, channels = field.shape
    cells = rows * cols
    head_size = channels // HEADS
    per_tile = TILE // head_size
    lat, lon = lax.axis_index("lat"), lax.axis_index("lon")

    loads = [
        pltpu.make_async_copy(source, target, load_sems.at[index])
        for index, (source, target) in enumerate(
            (
                (field_hbm, field),
                (taps_hbm, taps),
                (lon_attn_hbm, lon_attn),
                (expand_hbm, expand),
                (reduce_hbm, reduce),
                (lat_attn_hbm, lat_attn),
            )
        )
    ]
    for load in loads:
        load.start()

    north, south = lax.rem(lat + lats - 1, lats), lax.rem(lat + 1, lats)
    west, east = lax.rem(lon + lons - 1, lons), lax.rem(lon + 1, lons)

    barrier = pltpu.get_barrier_semaphore()

    def greet(place):
        pl.semaphore_signal(barrier, inc=1, device_id=place, device_id_type=MESH)

    for place in ((north, west), (north, east), (south, west), (south, east)):
        greet(place)

    def greet_lat(step, carry):
        greet((lax.rem(lat + step, lats), lon))
        return carry

    def greet_lon(step, carry):
        greet((lat, lax.rem(lon + step, lons)))
        return carry

    lax.fori_loop(1, lats, greet_lat, 0)
    lax.fori_loop(1, lons, greet_lon, 0)

    loads[0].wait()
    edge_first[...] = field[:, :4]
    edge_last[...] = field[:, cols - 4 :]
    pl.semaphore_wait(barrier, 4 + lats - 1 + lons - 1)

    tail, head = pl.ds(rows - REACH, REACH), pl.ds(0, REACH)
    after, inner = pl.ds(rows + REACH, REACH), pl.ds(REACH, rows)
    halos = []
    for index, (source, target, place) in enumerate(
        (
            (edge_last, left.at[inner], (lat, east)),
            (edge_first, right.at[inner], (lat, west)),
            (field.at[tail], top, (south, lon)),
            (field.at[head], bottom, (north, lon)),
            (edge_last.at[tail], left.at[head], (south, east)),
            (edge_last.at[head], left.at[after], (north, east)),
            (edge_first.at[tail], right.at[head], (south, west)),
            (edge_first.at[head], right.at[after], (north, west)),
        )
    ):
        copy = pltpu.make_async_remote_copy(
            src_ref=source,
            dst_ref=target,
            send_sem=halo_send.at[index],
            recv_sem=halo_recv.at[index],
            device_id=place,
            device_id_type=MESH,
        )
        copy.start()
        halos.append(copy)

    def exchange(phase, source_of, target):
        axis_lat = phase < 2
        members, me = (lats, lat) if axis_lat else (lons, lon)

        def copy_to(source, slot, place):
            return pltpu.make_async_remote_copy(
                src_ref=source,
                dst_ref=slot,
                send_sem=group_send.at[phase],
                recv_sem=group_recv.at[phase],
                device_id=place,
                device_id_type=MESH,
            )

        def send(step, carry):
            other = lax.rem(me + step, members)
            place = (other, lon) if axis_lat else (lat, other)
            copy_to(source_of(other), target.at[me], place).start()
            return carry

        lax.fori_loop(1, members, send, 0)
        target[me] = source_of(me)[...]
        others = target.at[pl.ds(0, members - 1)]
        return copy_to(others, others, (lat, lon))

    loads[1].wait()
    taps_wide[...] = taps[...].astype(jnp.float32)
    padded[pl.ds(REACH, rows), 8 : 8 + cols] = wide(field)

    into, out_of = iotas((cells, cells))
    to_lon = (into // rows == out_of % cols) & (into % rows == out_of // cols)
    lon_packed = into // (rows * PACK) * PACK + into % PACK
    lat_packed = into // PACK % rows
    pack = out_of == lat_packed * cols + lon_packed
    pack_lon = out_of == lon_packed * rows + lat_packed
    lon_unpacked = out_of // (rows * PACK) * PACK + out_of % PACK
    unpack = into == (out_of // PACK % rows) * cols + lon_unpacked
    for index, chosen in enumerate((to_lon, pack, pack_lon, unpack)):
        orders[index] = chosen.astype(jnp.float32).astype(jnp.bfloat16)
    loads[2].wait()
    loads[3].wait()
    loads[4].wait()
    loads[5].wait()

    for copy in halos:
        copy.wait_recv()
    not_first = (lat > 0).astype(jnp.float32)
    not_last = (lat < lats - 1).astype(jnp.float32)
    padded[pl.ds(0, REACH), 8 : 8 + cols] = wide(top) * not_first
    padded[pl.ds(rows + REACH, REACH), 8 : 8 + cols] = wide(bottom) * not_last
    for side, start in ((left, 4), (right, 8 + cols)):
        values = wide(side)
        padded[pl.ds(0, REACH), start : start + 4] = values[:REACH] * not_first
        padded[pl.ds(REACH, rows), start : start + 4] = values[REACH : REACH + rows]
        padded[pl.ds(rows + REACH, REACH), start : start + 4] = values[REACH + rows :] * not_last

    for half in range(channels // TILE):
        lanes = pl.ds(half * TILE, TILE)
        total = jnp.zeros((rows, cols, TILE), jnp.float32)
        for col_off in range(2 * REACH + 1):
            view = padded[:, 8 - REACH + col_off : 8 - REACH + col_off + cols, lanes]
            for row_off in range(2 * REACH + 1):
                tap = taps_wide[row_off, col_off : col_off + 1, lanes]
                total = total + view[row_off : row_off + rows] * tap
        convolved[:, lanes] = total.reshape(cells, TILE)

    normed = layer_norm(convolved[...]).astype(jnp.bfloat16)
    hidden = dot(normed, expand[...])
    hidden = 0.5 * hidden * (1.0 + lax.erf(hidden * (0.5**0.5)))
    own = field[...].astype(jnp.float32).reshape(cells, channels)
    block_one = (own + dot(hidden.astype(jnp.bfloat16), reduce[...])).astype(jnp.bfloat16)
    lat_in = layer_norm(block_one.astype(jnp.float32)).astype(jnp.bfloat16)

    by_lon = dot(orders[0], lat_in).astype(jnp.bfloat16)
    block_rows = cells // lats
    lat_out[...] = by_lon.reshape(lats, block_rows, channels)
    pending = exchange(0, lambda member: lat_out.at[member], lat_rows)
    block_packed[...] = dot(orders[1], block_one)
    pending.wait_recv()

    column = lat_rows[...].reshape(cells, channels)
    scale = head_size ** (-0.5) * math.log2(math.e)
    queries = (dot(column, lat_attn[0]) * scale).astype(jnp.bfloat16)
    keys = dot(column, lat_attn[1]).astype(jnp.bfloat16)
    values = dot(column, lat_attn[2]).astype(jnp.bfloat16)
    lane = lax.broadcasted_iota(jnp.int32, (cells, channels), 1)
    query_row, key_row = iotas((cells, cells))
    same = query_row // rows % (block_rows // rows) == key_row // rows % (block_rows // rows)
    mixed = jnp.zeros((cells, channels), jnp.float32)
    for head_index in range(HEADS):
        mine = lane // head_size == head_index
        scores = dot_t(queries, jnp.where(mine, keys, jnp.zeros_like(keys)))
        scores = jnp.where(same, scores, -1e30)
        probs = jnp.exp2(scores - jnp.max(scores, axis=-1, keepdims=True))
        probs = probs / jnp.sum(probs, axis=-1, keepdims=True)
        mixed = mixed + dot(
            probs.astype(jnp.bfloat16), jnp.where(mine, values, jnp.zeros_like(values))
        )
    lat_mix_out[...] = mixed.astype(jnp.bfloat16).reshape(lats, block_rows, channels)
    pending.wait_send()
    pending = exchange(1, lambda member: lat_mix_out.at[member], lat_mix_rows)
    pending.wait_recv()

    lat_mix = dot(orders[2], lat_mix_rows[...].reshape(cells, channels)).astype(jnp.bfloat16)
    block_two = (block_packed[...] + dot(lat_mix, lat_attn[3])).astype(jnp.bfloat16)
    block_packed[...] = block_two.astype(jnp.float32)
    lon_in = layer_norm(block_two.astype(jnp.float32)).astype(jnp.bfloat16)
    part = rows * PACK
    spot = lax.broadcasted_iota(jnp.int32, (part, TILE), 1) // head_size
    for kind in range(3):
        projected = dot(lon_in, lon_attn[kind])
        if kind == 0:
            projected = projected * scale
        for head_index in range(HEADS):
            tile, spot_from = head_index // per_tile * TILE, head_index % per_tile
            block = None
            for spot_to in range(per_tile):
                piece = projected[spot_to * part : (spot_to + 1) * part, tile : tile + TILE]
                if spot_to != spot_from:
                    piece = pltpu.roll(piece, (spot_to - spot_from) * head_size % TILE, 1)
                block = piece if block is None else jnp.where(spot == spot_to, piece, block)
            block = block.astype(jnp.bfloat16)
            lon_out[:, head_index, kind] = block.reshape(rows, PACK, TILE)
    pending.wait_send()
    pending = exchange(
        2, lambda member: lon_out.at[member // HEADS, lax.rem(member, HEADS)], lon_rows
    )
    pending.wait_recv()

    length = lons * cols
    packed_rows = length // per_tile
    source, target = iotas((TILE, per_tile * TILE))
    spread = target % TILE < head_size
    spread = spread & (source == target // TILE * head_size + target % TILE)
    spread = spread.astype(jnp.float32).astype(jnp.bfloat16)

    def apart(packed):
        return dot(packed, spread).astype(jnp.bfloat16)

    def stacked(parts):
        return jnp.concatenate(
            [parts[:, index * TILE : (index + 1) * TILE] for index in range(per_tile)], axis=0
        )

    keys = stacked(apart(lon_rows[:, 1].reshape(packed_rows, TILE)))
    values = stacked(apart(lon_rows[:, 2].reshape(packed_rows, TILE)))
    values = jnp.concatenate([values, jnp.ones((length, TILE), jnp.bfloat16)], axis=1)
    queries = apart(lon_rows[:, 0].reshape(packed_rows, TILE))
    sources = 16
    chunk = sources * PACK
    for start in range(0, packed_rows, chunk):
        scores = dot_t(stacked(queries[start : start + chunk]), keys)
        probs = jnp.exp2(scores - jnp.max(scores, axis=-1, keepdims=True))
        mixed = dot(probs.astype(jnp.bfloat16), values)
        mixed = mixed[:, :TILE] / mixed[:, TILE:]
        block = mixed[:chunk]
        for index in range(1, per_tile):
            piece = mixed[index * chunk : (index + 1) * chunk]
            block = block + pltpu.roll(piece, index * head_size, 1)
        first = start // PACK
        lon_mix_out[first : first + sources] = block.astype(jnp.bfloat16).reshape(
            sources, PACK, TILE
        )
    pending.wait_send()
    pending = exchange(3, lambda member: lon_mix_out.at[member], lon_mix_rows)
    pending.wait_recv()

    result = block_packed[...]
    for tile in range(channels // TILE):
        heads = [
            jnp.concatenate(
                [
                    lon_mix_rows[row_index * HEADS + head_index]
                    for row_index in range(rows)
                ],
                axis=0,
            ).astype(jnp.float32)
            for head_index in range(per_tile * tile, per_tile * (tile + 1))
        ]
        parts = []
        for spot_from in range(per_tile):
            block = None
            for spot_to in range(per_tile):
                piece = heads[spot_to]
                if spot_to != spot_from:
                    piece = pltpu.roll(piece, (spot_to - spot_from) * head_size % TILE, 1)
                block = piece if block is None else jnp.where(spot == spot_to, piece, block)
            parts.append(block)
        mixture = jnp.concatenate(parts, axis=0).astype(jnp.bfloat16)
        result = result + dot(mixture, lon_attn[3, tile * TILE : (tile + 1) * TILE])
    result = dot(orders[3], result.astype(jnp.bfloat16)).astype(jnp.bfloat16)
    out_ref[...] = result.reshape(rows, cols, channels)
    pending.wait_send()
    for copy in halos:
        copy.wait_send()


def shards(lats, lons, field, dw_weight, w_expand, w_reduce, lat_attn, lon_attn):
    rows, cols, channels = field.shape
    cells = rows * cols
    bf16, f32 = jnp.bfloat16, jnp.float32
    arguments = (field, dw_weight, w_expand, w_reduce, lat_attn, lon_attn)
    vmem = pltpu.VMEM
    edge = vmem((rows, 4, channels), bf16)
    strip = vmem((REACH, cols, channels), bf16)
    side = vmem((rows + 2 * REACH, 4, channels), bf16)
    column = vmem((lats, cells // lats, channels), bf16)
    mix = vmem((lons, PACK, TILE), bf16)
    return pl.pallas_call(
        functools.partial(kernel, lats, lons),
        out_shape=jax.ShapeDtypeStruct(field.shape, field.dtype),
        in_specs=[pl.BlockSpec(memory_space=pltpu.HBM)] * len(arguments),
        out_specs=pl.BlockSpec(memory_space=pltpu.VMEM),
        scratch_shapes=[
            *(vmem(argument.shape, argument.dtype) for argument in arguments),
            edge,
            edge,
            strip,
            strip,
            side,
            side,
            vmem((rows + 2 * REACH, cols + 16, channels), f32),
            vmem(dw_weight.shape, f32),
            vmem((cells, channels), f32),
            vmem((4, cells, cells), bf16),
            vmem((cells, channels), f32),
            column,
            column,
            column,
            column,
            vmem((rows, HEADS, 3, PACK, TILE), bf16),
            vmem((lons, 3, PACK, TILE), bf16),
            mix,
            mix,
            pltpu.SemaphoreType.DMA((len(arguments),)),
            pltpu.SemaphoreType.DMA((8,)),
            pltpu.SemaphoreType.DMA((8,)),
            pltpu.SemaphoreType.DMA((4,)),
            pltpu.SemaphoreType.DMA((4,)),
        ],
        compiler_params=pltpu.CompilerParams(
            collective_id=0, has_side_effects=True, vmem_limit_bytes=60 << 20
        ),
        name="block",
    )(*arguments)


def solution(mesh):
    return jax.shard_map(
        functools.partial(shards, mesh.shape["lat"], mesh.shape["lon"]),
        mesh=mesh,
        in_specs=(P("lat", "lon", None), P(), P(), P(), P(), P()),
        out_specs=P("lat", "lon", None),
        check_vma=False,
    )
```

```python
import functools
import math

import jax
import jax.numpy as jnp
from jax import lax
from jax.experimental import pallas as pl
from jax.experimental.pallas import tpu as pltpu
from jax.sharding import PartitionSpec as P

HEADS = 8
EPSILON = 1e-06
REACH = 3
TILE = 128
PACK = 4
SPANS = (2, 8, 4)
MESH = pl.DeviceIdType.MESH


def layer_norm(values):
    average = jnp.mean(values, axis=-1, keepdims=True)
    centered = values - average
    variance = jnp.mean(centered * centered, axis=-1, keepdims=True)
    return centered * lax.rsqrt(variance + EPSILON)


def dot(left, right):
    return jnp.dot(left, right, preferred_element_type=jnp.float32)


def dot_t(left, right):
    return lax.dot_general(left, right, (((1,), (1,)), ((), ())), preferred_element_type=jnp.float32)


def iotas(shape):
    return (lax.broadcasted_iota(jnp.int32, shape, 0), lax.broadcasted_iota(jnp.int32, shape, 1))


def far_first(step, members):
    return members // 2 + (step + 1) // 2 * (1 - 2 * (step % 2))


def wide(ref):
    return ref[...].astype(jnp.float32)


def kernel(
    lats,
    lons,
    field_hbm,
    taps_hbm,
    expand_hbm,
    reduce_hbm,
    lat_attn_hbm,
    lon_attn_hbm,
    out_ref,
    field,
    taps,
    expand,
    reduce,
    lat_attn,
    lon_attn,
    edge_first,
    edge_last,
    top,
    bottom,
    left,
    right,
    padded,
    taps_wide,
    convolved,
    orders,
    block_packed,
    lat_out,
    lat_rows,
    lat_mix_out,
    lat_mix_rows,
    lon_out,
    lon_rows,
    lon_mix_out,
    lon_mix_rows,
    load_sems,
    halo_send,
    halo_recv,
    group_send,
    group_recv,
    ready_sems,
):
    rows, cols, channels = field.shape
    cells = rows * cols
    head_size = channels // HEADS
    per_tile = TILE // head_size
    lat, lon = lax.axis_index("lat"), lax.axis_index("lon")

    loads = [
        pltpu.make_async_copy(source, target, load_sems.at[index])
        for index, (source, target) in enumerate(
            (
                (field_hbm, field),
                (taps_hbm, taps),
                (lon_attn_hbm, lon_attn),
                (expand_hbm, expand),
                (reduce_hbm, reduce),
                (lat_attn_hbm, lat_attn),
            )
        )
    ]
    for load in loads:
        load.start()

    north, south = lax.rem(lat + lats - 1, lats), lax.rem(lat + 1, lats)
    west, east = lax.rem(lon + lons - 1, lons), lax.rem(lon + 1, lons)

    barrier = pltpu.get_barrier_semaphore()

    def greet(place):
        pl.semaphore_signal(barrier, inc=1, device_id=place, device_id_type=MESH)

    plane, line, column_place = lon // (SPANS[1] * SPANS[2]), lon // SPANS[2] % SPANS[1], lon % SPANS[2]

    def shifted(dz, dy, dx):
        return (
            lax.rem(plane + dz, SPANS[0]) * SPANS[1] * SPANS[2]
            + lax.rem(line + dy, SPANS[1]) * SPANS[2]
            + lax.rem(column_place + dx, SPANS[2])
        )

    for step in range(SPANS[1] - 1):
        greet((lat, shifted(0, far_first(step, SPANS[1]), 0)))
    for step in range(lats - 1):
        greet((lax.rem(lat + far_first(step, lats), lats), lon))
    for place in ((north, west), (north, east), (south, west), (south, east)):
        greet(place)
    greet((lat, west))
    greet((lat, east))
    greet((lat, shifted(1, 0, 0)))
    for step in range(1, SPANS[2]):
        greet((lat, shifted(0, 0, step)))

    loads[0].wait()
    edge_first[...] = field[:, :4]
    edge_last[...] = field[:, cols - 4 :]
    pl.semaphore_wait(barrier, lats - 1 + 4 + 2 + sum(SPANS) - len(SPANS))

    tail, head = pl.ds(rows - REACH, REACH), pl.ds(0, REACH)
    after, inner = pl.ds(rows + REACH, REACH), pl.ds(REACH, rows)
    halos = []
    for index, (source, target, place) in enumerate(
        (
            (edge_last, left.at[inner], (lat, east)),
            (edge_first, right.at[inner], (lat, west)),
            (field.at[tail], top, (south, lon)),
            (field.at[head], bottom, (north, lon)),
            (edge_last.at[tail], left.at[head], (south, east)),
            (edge_last.at[head], left.at[after], (north, east)),
            (edge_first.at[tail], right.at[head], (south, west)),
            (edge_first.at[head], right.at[after], (north, west)),
        )
    ):
        copy = pltpu.make_async_remote_copy(
            src_ref=source,
            dst_ref=target,
            send_sem=halo_send.at[index],
            recv_sem=halo_recv.at[index],
            device_id=place,
            device_id_type=MESH,
        )
        copy.start()
        halos.append(copy)

    def ready(index, place):
        pl.semaphore_signal(
            ready_sems.at[index], inc=1, device_id=place, device_id_type=MESH
        )

    for step in range(1, SPANS[2]):
        ready(0, (lat, shifted(0, 0, step)))

    def copy_to(phase, source, slot, place):
        return pltpu.make_async_remote_copy(
            src_ref=source,
            dst_ref=slot,
            send_sem=group_send.at[phase],
            recv_sem=group_recv.at[phase],
            device_id=place,
            device_id_type=MESH,
        )

    def all_of(phase, target, members):
        others = target.at[pl.ds(0, members - 1)]
        return copy_to(phase, others, others, (lat, lon))

    def exchange_lat(phase, source, target):
        def send(step, carry):
            other = lax.rem(lat + far_first(step, lats), lats)
            copy_to(phase, source.at[other], target.at[lat], (other, lon)).start()
            return carry

        lax.fori_loop(0, lats - 1, send, 0)
        target[lat] = source[lat]
        return all_of(phase, target, lats)

    loads[1].wait()
    taps_wide[...] = taps[...].astype(jnp.float32)
    padded[pl.ds(REACH, rows), 8 : 8 + cols] = wide(field)

    into, out_of = iotas((cells, cells))
    to_lon = (into // rows == out_of % cols) & (into % rows == out_of // cols)
    lon_packed = into // (rows * PACK) * PACK + into % PACK
    lat_packed = into // PACK % rows
    pack = out_of == lat_packed * cols + lon_packed
    pack_lon = out_of == lon_packed * rows + lat_packed
    lon_unpacked = out_of // (rows * PACK) * PACK + out_of % PACK
    unpack = into == (out_of // PACK % rows) * cols + lon_unpacked
    for index, chosen in enumerate((to_lon, pack, pack_lon, unpack)):
        orders[index] = chosen.astype(jnp.float32).astype(jnp.bfloat16)
    loads[2].wait()
    loads[3].wait()
    loads[4].wait()
    loads[5].wait()

    for copy in halos:
        copy.wait_recv()
    pl.semaphore_wait(ready_sems.at[0], SPANS[2] - 1)
    ready(1, (lat, shifted(1, 0, 0)))
    not_first = (lat > 0).astype(jnp.float32)
    not_last = (lat < lats - 1).astype(jnp.float32)
    padded[pl.ds(0, REACH), 8 : 8 + cols] = wide(top) * not_first
    padded[pl.ds(rows + REACH, REACH), 8 : 8 + cols] = wide(bottom) * not_last
    for side, start in ((left, 4), (right, 8 + cols)):
        values = wide(side)
        padded[pl.ds(0, REACH), start : start + 4] = values[:REACH] * not_first
        padded[pl.ds(REACH, rows), start : start + 4] = values[REACH : REACH + rows]
        padded[pl.ds(rows + REACH, REACH), start : start + 4] = values[REACH + rows :] * not_last

    for half in range(channels // TILE):
        lanes = pl.ds(half * TILE, TILE)
        total = jnp.zeros((rows, cols, TILE), jnp.float32)
        for col_off in range(2 * REACH + 1):
            view = padded[:, 8 - REACH + col_off : 8 - REACH + col_off + cols, lanes]
            for row_off in range(2 * REACH + 1):
                tap = taps_wide[row_off, col_off : col_off + 1, lanes]
                total = total + view[row_off : row_off + rows] * tap
        convolved[:, lanes] = total.reshape(cells, TILE)

    normed = layer_norm(convolved[...]).astype(jnp.bfloat16)
    hidden = dot(normed, expand[...])
    hidden = 0.5 * hidden * (1.0 + lax.erf(hidden * (0.5**0.5)))
    own = field[...].astype(jnp.float32).reshape(cells, channels)
    block_one = (own + dot(hidden.astype(jnp.bfloat16), reduce[...])).astype(jnp.bfloat16)
    lat_in = layer_norm(block_one.astype(jnp.float32)).astype(jnp.bfloat16)

    by_lon = dot(orders[0], lat_in).astype(jnp.bfloat16)
    block_rows = cells // lats
    lat_out[...] = by_lon.reshape(lats, block_rows, channels)
    pending = exchange_lat(0, lat_out, lat_rows)
    block_packed[...] = dot(orders[1], block_one)
    pending.wait_recv()

    column = lat_rows[...].reshape(cells, channels)
    scale = head_size ** (-0.5) * math.log2(math.e)
    queries = (dot(column, lat_attn[0]) * scale).astype(jnp.bfloat16)
    keys = dot(column, lat_attn[1]).astype(jnp.bfloat16)
    values = dot(column, lat_attn[2]).astype(jnp.bfloat16)
    lane = lax.broadcasted_iota(jnp.int32, (cells, channels), 1)
    query_row, key_row = iotas((cells, cells))
    same = query_row // rows % (block_rows // rows) == key_row // rows % (block_rows // rows)
    mixed = jnp.zeros((cells, channels), jnp.float32)
    for head_index in range(HEADS):
        mine = lane // head_size == head_index
        scores = dot_t(queries, jnp.where(mine, keys, jnp.zeros_like(keys)))
        scores = jnp.where(same, scores, -1e30)
        probs = jnp.exp2(scores - jnp.max(scores, axis=-1, keepdims=True))
        probs = probs / jnp.sum(probs, axis=-1, keepdims=True)
        mixed = mixed + dot(
            probs.astype(jnp.bfloat16), jnp.where(mine, values, jnp.zeros_like(values))
        )
    lat_mix_out[...] = mixed.astype(jnp.bfloat16).reshape(lats, block_rows, channels)
    pending.wait_send()
    pending = exchange_lat(1, lat_mix_out, lat_mix_rows)
    pending.wait_recv()

    lat_mix = dot(orders[2], lat_mix_rows[...].reshape(cells, channels)).astype(jnp.bfloat16)
    block_two = (block_packed[...] + dot(lat_mix, lat_attn[3])).astype(jnp.bfloat16)
    block_packed[...] = block_two.astype(jnp.float32)
    lon_in = layer_norm(block_two.astype(jnp.float32)).astype(jnp.bfloat16)
    part = rows * PACK
    spot = lax.broadcasted_iota(jnp.int32, (part, TILE), 1) // head_size
    for kind in range(3):
        projected = dot(lon_in, lon_attn[kind])
        if kind == 0:
            projected = projected * scale
        for head_index in range(HEADS):
            tile, spot_from = head_index // per_tile * TILE, head_index % per_tile
            block = None
            for spot_to in range(per_tile):
                piece = projected[spot_to * part : (spot_to + 1) * part, tile : tile + TILE]
                if spot_to != spot_from:
                    piece = pltpu.roll(piece, (spot_to - spot_from) * head_size % TILE, 1)
                block = piece if block is None else jnp.where(spot == spot_to, piece, block)
            block = block.astype(jnp.bfloat16)
            lon_out[:, head_index, kind] = block.reshape(rows, PACK, TILE)
    pending.wait_send()
    pl.semaphore_wait(ready_sems.at[1], 1)

    def send_row(step, carry):
        other = shifted(
            1 - step % 2,
            far_first(step // (SPANS[0] * SPANS[2]), SPANS[1]),
            far_first(step // SPANS[0] % SPANS[2], SPANS[2]),
        )
        source = lon_out.at[other // HEADS, lax.rem(other, HEADS)]
        copy_to(2, source, lon_rows.at[lon], (lat, other)).start()
        return carry

    lax.fori_loop(0, lons - 1, send_row, 0)
    lon_rows[lon] = lon_out[lon // HEADS, lax.rem(lon, HEADS)]
    pending = all_of(2, lon_rows, lons)
    pending.wait_recv()

    length = lons * cols
    packed_rows = length // per_tile
    source, target = iotas((TILE, per_tile * TILE))
    spread = target % TILE < head_size
    spread = spread & (source == target // TILE * head_size + target % TILE)
    spread = spread.astype(jnp.float32).astype(jnp.bfloat16)

    def apart(packed):
        return dot(packed, spread).astype(jnp.bfloat16)

    def stacked(parts):
        return jnp.concatenate(
            [parts[:, index * TILE : (index + 1) * TILE] for index in range(per_tile)], axis=0
        )

    keys = stacked(apart(lon_rows[:, 1].reshape(packed_rows, TILE)))
    values = stacked(apart(lon_rows[:, 2].reshape(packed_rows, TILE)))
    values = jnp.concatenate([values, jnp.ones((length, TILE), jnp.bfloat16)], axis=1)
    pending.wait_send()
    per_step = 2
    run = SPANS[2] * PACK
    for step in range(0, SPANS[1], per_step):
        offsets = [
            (dz, far_first(step + index, SPANS[1])) for index in range(per_step) for dz in (1, 0)
        ]
        firsts = [shifted(dz, dy, 0) - column_place for dz, dy in offsets]
        queries = [
            lon_rows[pl.ds(first, SPANS[2]), 0].reshape(run, TILE) for first in firsts
        ]
        queries = apart(jnp.concatenate(queries, axis=0))
        scores = dot_t(stacked(queries), keys)
        probs = jnp.exp2(scores - jnp.max(scores, axis=-1, keepdims=True))
        mixed = dot(probs.astype(jnp.bfloat16), values)
        mixed = mixed[:, :TILE] / mixed[:, TILE:]
        chunk = run * len(offsets)
        block = mixed[:chunk]
        for index in range(1, per_tile):
            piece = mixed[index * chunk : (index + 1) * chunk]
            block = block + pltpu.roll(piece, index * head_size, 1)
        block = block.astype(jnp.bfloat16)
        for index, (first, (dz, dy)) in enumerate(zip(firsts, offsets)):
            lon_mix_out[pl.ds(first, SPANS[2])] = block[index * run : (index + 1) * run].reshape(
                SPANS[2], PACK, TILE
            )
        for dz, dy in offsets:
            for dx in (2, 1, 3, 0):
                if (dz, dy, dx) != (0, 0, 0):
                    other = shifted(dz, dy, dx)
                    copy_to(3, lon_mix_out.at[other], lon_mix_rows.at[lon], (lat, other)).start()
    lon_mix_rows[lon] = lon_mix_out[lon]
    pending = all_of(3, lon_mix_rows, lons)
    pending.wait_recv()

    result = block_packed[...]
    for tile in range(channels // TILE):
        heads = [
            jnp.concatenate(
                [
                    lon_mix_rows[row_index * HEADS + head_index]
                    for row_index in range(rows)
                ],
                axis=0,
            ).astype(jnp.float32)
            for head_index in range(per_tile * tile, per_tile * (tile + 1))
        ]
        parts = []
        for spot_from in range(per_tile):
            block = None
            for spot_to in range(per_tile):
                piece = heads[spot_to]
                if spot_to != spot_from:
                    piece = pltpu.roll(piece, (spot_to - spot_from) * head_size % TILE, 1)
                block = piece if block is None else jnp.where(spot == spot_to, piece, block)
            parts.append(block)
        mixture = jnp.concatenate(parts, axis=0).astype(jnp.bfloat16)
        result = result + dot(mixture, lon_attn[3, tile * TILE : (tile + 1) * TILE])
    result = dot(orders[3], result.astype(jnp.bfloat16)).astype(jnp.bfloat16)
    out_ref[...] = result.reshape(rows, cols, channels)
    pending.wait_send()
    for copy in halos:
        copy.wait_send()


def shards(lats, lons, field, dw_weight, w_expand, w_reduce, lat_attn, lon_attn):
    rows, cols, channels = field.shape
    cells = rows * cols
    bf16, f32 = jnp.bfloat16, jnp.float32
    arguments = (field, dw_weight, w_expand, w_reduce, lat_attn, lon_attn)
    vmem = pltpu.VMEM
    edge = vmem((rows, 4, channels), bf16)
    strip = vmem((REACH, cols, channels), bf16)
    side = vmem((rows + 2 * REACH, 4, channels), bf16)
    column = vmem((lats, cells // lats, channels), bf16)
    mix = vmem((lons, PACK, TILE), bf16)
    return pl.pallas_call(
        functools.partial(kernel, lats, lons),
        out_shape=jax.ShapeDtypeStruct(field.shape, field.dtype),
        in_specs=[pl.BlockSpec(memory_space=pltpu.HBM)] * len(arguments),
        out_specs=pl.BlockSpec(memory_space=pltpu.VMEM),
        scratch_shapes=[
            *(vmem(argument.shape, argument.dtype) for argument in arguments),
            edge,
            edge,
            strip,
            strip,
            side,
            side,
            vmem((rows + 2 * REACH, cols + 16, channels), f32),
            vmem(dw_weight.shape, f32),
            vmem((cells, channels), f32),
            vmem((4, cells, cells), bf16),
            vmem((cells, channels), f32),
            column,
            column,
            column,
            column,
            vmem((rows, HEADS, 3, PACK, TILE), bf16),
            vmem((lons, 3, PACK, TILE), bf16),
            mix,
            mix,
            pltpu.SemaphoreType.DMA((len(arguments),)),
            pltpu.SemaphoreType.DMA((8,)),
            pltpu.SemaphoreType.DMA((8,)),
            pltpu.SemaphoreType.DMA((4,)),
            pltpu.SemaphoreType.DMA((4,)),
            pltpu.SemaphoreType.REGULAR((2,)),
        ],
        compiler_params=pltpu.CompilerParams(
            collective_id=0, has_side_effects=True, vmem_limit_bytes=48 << 20
        ),
        name="block",
    )(*(pltpu.with_memory_space_constraint(argument, pltpu.HBM) for argument in arguments))


def solution(mesh):
    return jax.shard_map(
        functools.partial(shards, mesh.shape["lat"], mesh.shape["lon"]),
        mesh=mesh,
        in_specs=(P("lat", "lon", None), P(), P(), P(), P(), P()),
        out_specs=P("lat", "lon", None),
        check_vma=False,
    )
```

```python
import functools
import math

import jax
import jax.numpy as jnp
from jax import lax
from jax.experimental import pallas as pl
from jax.experimental.pallas import tpu as pltpu
from jax.sharding import PartitionSpec as P

HEADS = 8
EPSILON = 1e-06
REACH = 3
TILE = 128
PACK = 4
SPANS = (2, 8, 4)
MESH = pl.DeviceIdType.MESH


def layer_norm(values):
    average = jnp.mean(values, axis=-1, keepdims=True)
    centered = values - average
    variance = jnp.mean(centered * centered, axis=-1, keepdims=True)
    return centered * lax.rsqrt(variance + EPSILON)


def dot(left, right):
    return jnp.dot(left, right, preferred_element_type=jnp.float32)


def dot_t(left, right):
    return lax.dot_general(left, right, (((1,), (1,)), ((), ())), preferred_element_type=jnp.float32)


def iotas(shape):
    return (lax.broadcasted_iota(jnp.int32, shape, 0), lax.broadcasted_iota(jnp.int32, shape, 1))


def far_first(step, members):
    return members // 2 + (step + 1) // 2 * (1 - 2 * (step % 2))


def wide(ref):
    return ref[...].astype(jnp.float32)


def kernel(
    lats,
    lons,
    field_hbm,
    taps_hbm,
    expand_hbm,
    reduce_hbm,
    lat_attn_hbm,
    lon_attn_hbm,
    out_ref,
    field,
    taps,
    expand,
    reduce,
    lat_attn,
    lon_attn,
    edge_first,
    edge_last,
    top,
    bottom,
    left,
    right,
    padded,
    taps_wide,
    convolved,
    orders,
    block_packed,
    lat_out,
    lat_rows,
    lat_mix_out,
    lat_mix_rows,
    lon_out,
    lon_rows,
    lon_mix_out,
    lon_mix_rows,
    lon_queries,
    load_sems,
    halo_send,
    halo_recv,
    group_send,
    group_recv,
    ready_sems,
):
    rows, cols, channels = field.shape
    cells = rows * cols
    head_size = channels // HEADS
    per_tile = TILE // head_size
    lat, lon = lax.axis_index("lat"), lax.axis_index("lon")

    loads = [
        pltpu.make_async_copy(source, target, load_sems.at[index])
        for index, (source, target) in enumerate(
            (
                (field_hbm, field),
                (taps_hbm, taps),
                (lon_attn_hbm, lon_attn),
                (expand_hbm, expand),
                (reduce_hbm, reduce),
                (lat_attn_hbm, lat_attn),
            )
        )
    ]
    for load in loads:
        load.start()

    north, south = lax.rem(lat + lats - 1, lats), lax.rem(lat + 1, lats)
    west, east = lax.rem(lon + lons - 1, lons), lax.rem(lon + 1, lons)

    barrier = pltpu.get_barrier_semaphore()

    def greet(place):
        pl.semaphore_signal(barrier, inc=1, device_id=place, device_id_type=MESH)

    plane, line, column_place = lon // (SPANS[1] * SPANS[2]), lon // SPANS[2] % SPANS[1], lon % SPANS[2]

    def shifted(dz, dy, dx):
        return (
            lax.rem(plane + dz, SPANS[0]) * SPANS[1] * SPANS[2]
            + lax.rem(line + dy, SPANS[1]) * SPANS[2]
            + lax.rem(column_place + dx, SPANS[2])
        )

    for step in range(SPANS[1] - 1):
        greet((lat, shifted(0, far_first(step, SPANS[1]), 0)))
    for step in range(lats - 1):
        greet((lax.rem(lat + far_first(step, lats), lats), lon))
    for place in ((north, west), (north, east), (south, west), (south, east)):
        greet(place)
    greet((lat, west))
    greet((lat, east))
    greet((lat, shifted(1, 0, 0)))
    for step in range(1, SPANS[2]):
        greet((lat, shifted(0, 0, step)))

    loads[0].wait()
    edge_first[...] = field[:, :4]
    edge_last[...] = field[:, cols - 4 :]
    pl.semaphore_wait(barrier, lats - 1 + 4 + 2 + sum(SPANS) - len(SPANS))

    tail, head = pl.ds(rows - REACH, REACH), pl.ds(0, REACH)
    after, inner = pl.ds(rows + REACH, REACH), pl.ds(REACH, rows)
    halos = []
    for index, (source, target, place) in enumerate(
        (
            (edge_last, left.at[inner], (lat, east)),
            (edge_first, right.at[inner], (lat, west)),
            (field.at[tail], top, (south, lon)),
            (field.at[head], bottom, (north, lon)),
            (edge_last.at[tail], left.at[head], (south, east)),
            (edge_last.at[head], left.at[after], (north, east)),
            (edge_first.at[tail], right.at[head], (south, west)),
            (edge_first.at[head], right.at[after], (north, west)),
        )
    ):
        copy = pltpu.make_async_remote_copy(
            src_ref=source,
            dst_ref=target,
            send_sem=halo_send.at[index],
            recv_sem=halo_recv.at[index],
            device_id=place,
            device_id_type=MESH,
        )
        copy.start()
        halos.append(copy)

    def ready(index, place):
        pl.semaphore_signal(
            ready_sems.at[index], inc=1, device_id=place, device_id_type=MESH
        )

    for step in range(1, SPANS[2]):
        ready(0, (lat, shifted(0, 0, step)))

    def copy_to(phase, source, slot, place):
        return pltpu.make_async_remote_copy(
            src_ref=source,
            dst_ref=slot,
            send_sem=group_send.at[phase],
            recv_sem=group_recv.at[phase],
            device_id=place,
            device_id_type=MESH,
        )

    def all_of(phase, target, members):
        others = target.at[pl.ds(0, members - 1)]
        return copy_to(phase, others, others, (lat, lon))

    def exchange_lat(phase, source, target):
        def send(step, carry):
            other = lax.rem(lat + far_first(step, lats), lats)
            copy_to(phase, source.at[other], target.at[lat], (other, lon)).start()
            return carry

        lax.fori_loop(0, lats - 1, send, 0)
        target[lat] = source[lat]
        return all_of(phase, target, lats)

    loads[1].wait()
    taps_wide[...] = taps[...].astype(jnp.float32)
    padded[pl.ds(REACH, rows), 8 : 8 + cols] = wide(field)

    into, out_of = iotas((cells, cells))
    to_lon = (into // rows == out_of % cols) & (into % rows == out_of // cols)
    lon_packed = into // (rows * PACK) * PACK + into % PACK
    lat_packed = into // PACK % rows
    pack = out_of == lat_packed * cols + lon_packed
    pack_lon = out_of == lon_packed * rows + lat_packed
    lon_unpacked = out_of // (rows * PACK) * PACK + out_of % PACK
    unpack = into == (out_of // PACK % rows) * cols + lon_unpacked
    for index, chosen in enumerate((to_lon, pack, pack_lon, unpack)):
        orders[index] = chosen.astype(jnp.float32).astype(jnp.bfloat16)
    loads[2].wait()
    loads[3].wait()
    loads[4].wait()
    loads[5].wait()

    for copy in halos:
        copy.wait_recv()
    pl.semaphore_wait(ready_sems.at[0], SPANS[2] - 1)
    ready(1, (lat, shifted(1, 0, 0)))
    not_first = (lat > 0).astype(jnp.float32)
    not_last = (lat < lats - 1).astype(jnp.float32)
    padded[pl.ds(0, REACH), 8 : 8 + cols] = wide(top) * not_first
    padded[pl.ds(rows + REACH, REACH), 8 : 8 + cols] = wide(bottom) * not_last
    for side, start in ((left, 4), (right, 8 + cols)):
        values = wide(side)
        padded[pl.ds(0, REACH), start : start + 4] = values[:REACH] * not_first
        padded[pl.ds(REACH, rows), start : start + 4] = values[REACH : REACH + rows]
        padded[pl.ds(rows + REACH, REACH), start : start + 4] = values[REACH + rows :] * not_last

    for half in range(channels // TILE):
        lanes = pl.ds(half * TILE, TILE)
        total = jnp.zeros((rows, cols, TILE), jnp.float32)
        for col_off in range(2 * REACH + 1):
            view = padded[:, 8 - REACH + col_off : 8 - REACH + col_off + cols, lanes]
            for row_off in range(2 * REACH + 1):
                tap = taps_wide[row_off, col_off : col_off + 1, lanes]
                total = total + view[row_off : row_off + rows] * tap
        convolved[:, lanes] = total.reshape(cells, TILE)

    normed = layer_norm(convolved[...]).astype(jnp.bfloat16)
    hidden = dot(normed, expand[...])
    hidden = 0.5 * hidden * (1.0 + lax.erf(hidden * (0.5**0.5)))
    own = field[...].astype(jnp.float32).reshape(cells, channels)
    block_one = (own + dot(hidden.astype(jnp.bfloat16), reduce[...])).astype(jnp.bfloat16)
    lat_in = layer_norm(block_one.astype(jnp.float32)).astype(jnp.bfloat16)

    by_lon = dot(orders[0], lat_in).astype(jnp.bfloat16)
    block_rows = cells // lats
    lat_out[...] = by_lon.reshape(lats, block_rows, channels)
    pending = exchange_lat(0, lat_out, lat_rows)
    block_packed[...] = dot(orders[1], block_one)
    pending.wait_recv()

    column = lat_rows[...].reshape(cells, channels)
    scale = head_size ** (-0.5) * math.log2(math.e)
    queries = (dot(column, lat_attn[0]) * scale).astype(jnp.bfloat16)
    keys = dot(column, lat_attn[1]).astype(jnp.bfloat16)
    values = dot(column, lat_attn[2]).astype(jnp.bfloat16)
    lane = lax.broadcasted_iota(jnp.int32, (cells, channels), 1)
    query_row, key_row = iotas((cells, cells))
    same = query_row // rows % (block_rows // rows) == key_row // rows % (block_rows // rows)
    mixed = jnp.zeros((cells, channels), jnp.float32)
    for head_index in range(HEADS):
        mine = lane // head_size == head_index
        scores = dot_t(queries, jnp.where(mine, keys, jnp.zeros_like(keys)))
        scores = jnp.where(same, scores, -1e30)
        probs = jnp.exp2(scores - jnp.max(scores, axis=-1, keepdims=True))
        probs = probs / jnp.sum(probs, axis=-1, keepdims=True)
        mixed = mixed + dot(
            probs.astype(jnp.bfloat16), jnp.where(mine, values, jnp.zeros_like(values))
        )
    lat_mix_out[...] = mixed.astype(jnp.bfloat16).reshape(lats, block_rows, channels)
    pending.wait_send()
    pending = exchange_lat(1, lat_mix_out, lat_mix_rows)
    pending.wait_recv()

    lat_mix = dot(orders[2], lat_mix_rows[...].reshape(cells, channels)).astype(jnp.bfloat16)
    block_two = (block_packed[...] + dot(lat_mix, lat_attn[3])).astype(jnp.bfloat16)
    block_packed[...] = block_two.astype(jnp.float32)
    lon_in = layer_norm(block_two.astype(jnp.float32)).astype(jnp.bfloat16)
    part = rows * PACK
    spot = lax.broadcasted_iota(jnp.int32, (part, TILE), 1) // head_size
    for kind in range(3):
        projected = dot(lon_in, lon_attn[kind])
        if kind == 0:
            projected = projected * scale
        projected = projected.astype(jnp.bfloat16)
        for head_index in range(HEADS):
            tile, spot_from = head_index // per_tile * TILE, head_index % per_tile
            block = None
            for spot_to in range(per_tile):
                piece = projected[spot_to * part : (spot_to + 1) * part, tile : tile + TILE]
                if spot_to != spot_from:
                    piece = pltpu.roll(piece, (spot_to - spot_from) * head_size % TILE, 1)
                block = piece if block is None else jnp.where(spot == spot_to, piece, block)
            lon_out[:, head_index, kind] = block.reshape(rows, PACK, TILE)
    pending.wait_send()
    pl.semaphore_wait(ready_sems.at[1], 1)

    def send_row(step, carry):
        other = shifted(
            1 - step % 2,
            far_first(step // (SPANS[0] * SPANS[2]), SPANS[1]),
            far_first(step // SPANS[0] % SPANS[2], SPANS[2]),
        )
        source = lon_out.at[other // HEADS, lax.rem(other, HEADS)]
        copy_to(2, source, lon_rows.at[lon], (lat, other)).start()
        return carry

    lax.fori_loop(0, lons - 1, send_row, 0)
    lon_rows[lon] = lon_out[lon // HEADS, lax.rem(lon, HEADS)]
    pending = all_of(2, lon_rows, lons)
    pending.wait_recv()

    length = lons * cols
    packed_rows = length // per_tile
    source, target = iotas((TILE, per_tile * TILE))
    spread = target % TILE < head_size
    spread = spread & (source == target // TILE * head_size + target % TILE)
    spread = spread.astype(jnp.float32).astype(jnp.bfloat16)

    def apart(packed):
        return dot(packed, spread).astype(jnp.bfloat16)

    def stacked(parts):
        return jnp.concatenate(
            [parts[:, index * TILE : (index + 1) * TILE] for index in range(per_tile)], axis=0
        )

    keys = stacked(apart(lon_rows[:, 1].reshape(packed_rows, TILE)))
    values = stacked(apart(lon_rows[:, 2].reshape(packed_rows, TILE)))
    values = jnp.concatenate([values, jnp.ones((length, TILE), jnp.bfloat16)], axis=1)
    pending.wait_send()
    spread_queries = apart(lon_rows[:, 0].reshape(packed_rows, TILE))
    for index in range(per_tile):
        lon_queries[index] = spread_queries[:, index * TILE : (index + 1) * TILE]
    per_step = 2
    run = SPANS[2] * PACK
    def prepare(step):
        offsets = [
            (dz, far_first(step + index, SPANS[1])) for index in range(per_step) for dz in (1, 0)
        ]
        firsts = [shifted(dz, dy, 0) - column_place for dz, dy in offsets]
        spots = [pl.ds(pl.multiple_of(first * PACK, run), run) for first in firsts]
        queries = jnp.concatenate(
            [lon_queries[index, rows_of] for index in range(per_tile) for rows_of in spots], axis=0
        )
        scores = dot_t(queries, keys)
        return scores, firsts, offsets

    upcoming = prepare(0)
    for step in range(0, SPANS[1], per_step):
        scores, firsts, offsets = upcoming
        if step + per_step < SPANS[1]:
            upcoming = prepare(step + per_step)
        probs = jnp.exp2(scores - jnp.max(scores, axis=-1, keepdims=True))
        mixed = dot(probs.astype(jnp.bfloat16), values)
        mixed = mixed[:, :TILE] / mixed[:, TILE:]
        chunk = run * len(offsets)
        block = mixed[:chunk]
        for index in range(1, per_tile):
            piece = mixed[index * chunk : (index + 1) * chunk]
            block = block + pltpu.roll(piece, index * head_size, 1)
        block = block.astype(jnp.bfloat16)
        for index, (first, (dz, dy)) in enumerate(zip(firsts, offsets)):
            lon_mix_out[pl.ds(first, SPANS[2])] = block[index * run : (index + 1) * run].reshape(
                SPANS[2], PACK, TILE
            )
        for dz, dy in offsets:
            for dx in (2, 1, 3, 0):
                if (dz, dy, dx) != (0, 0, 0):
                    other = shifted(dz, dy, dx)
                    copy_to(3, lon_mix_out.at[other], lon_mix_rows.at[lon], (lat, other)).start()
    lon_mix_rows[lon] = lon_mix_out[lon]
    pending = all_of(3, lon_mix_rows, lons)
    pending.wait_recv()

    result = block_packed[...]
    for tile in range(channels // TILE):
        heads = [
            jnp.concatenate(
                [
                    lon_mix_rows[row_index * HEADS + head_index]
                    for row_index in range(rows)
                ],
                axis=0,
            )
            for head_index in range(per_tile * tile, per_tile * (tile + 1))
        ]
        parts = []
        for spot_from in range(per_tile):
            block = None
            for spot_to in range(per_tile):
                piece = heads[spot_to]
                if spot_to != spot_from:
                    piece = pltpu.roll(piece, (spot_to - spot_from) * head_size % TILE, 1)
                block = piece if block is None else jnp.where(spot == spot_to, piece, block)
            parts.append(block)
        mixture = jnp.concatenate(parts, axis=0)
        result = result + dot(mixture, lon_attn[3, tile * TILE : (tile + 1) * TILE])
    result = dot(orders[3], result.astype(jnp.bfloat16)).astype(jnp.bfloat16)
    out_ref[...] = result.reshape(rows, cols, channels)
    pending.wait_send()
    for copy in halos:
        copy.wait_send()


def shards(lats, lons, field, dw_weight, w_expand, w_reduce, lat_attn, lon_attn):
    rows, cols, channels = field.shape
    cells = rows * cols
    bf16, f32 = jnp.bfloat16, jnp.float32
    arguments = (field, dw_weight, w_expand, w_reduce, lat_attn, lon_attn)
    vmem = pltpu.VMEM
    edge = vmem((rows, 4, channels), bf16)
    strip = vmem((REACH, cols, channels), bf16)
    side = vmem((rows + 2 * REACH, 4, channels), bf16)
    column = vmem((lats, cells // lats, channels), bf16)
    mix = vmem((lons, PACK, TILE), bf16)
    return pl.pallas_call(
        functools.partial(kernel, lats, lons),
        out_shape=jax.ShapeDtypeStruct(field.shape, field.dtype),
        in_specs=[pl.BlockSpec(memory_space=pltpu.HBM)] * len(arguments),
        out_specs=pl.BlockSpec(memory_space=pltpu.VMEM),
        scratch_shapes=[
            *(vmem(argument.shape, argument.dtype) for argument in arguments),
            edge,
            edge,
            strip,
            strip,
            side,
            side,
            vmem((rows + 2 * REACH, cols + 16, channels), f32),
            vmem(dw_weight.shape, f32),
            vmem((cells, channels), f32),
            vmem((4, cells, cells), bf16),
            vmem((cells, channels), f32),
            column,
            column,
            column,
            column,
            vmem((rows, HEADS, 3, PACK, TILE), bf16),
            vmem((lons, 3, PACK, TILE), bf16),
            mix,
            mix,
            vmem((TILE * HEADS // channels, lons * PACK, TILE), bf16),
            pltpu.SemaphoreType.DMA((len(arguments),)),
            pltpu.SemaphoreType.DMA((8,)),
            pltpu.SemaphoreType.DMA((8,)),
            pltpu.SemaphoreType.DMA((4,)),
            pltpu.SemaphoreType.DMA((4,)),
            pltpu.SemaphoreType.REGULAR((2,)),
        ],
        compiler_params=pltpu.CompilerParams(
            collective_id=0, has_side_effects=True, vmem_limit_bytes=48 << 20
        ),
        name="block",
    )(*(pltpu.with_memory_space_constraint(argument, pltpu.HBM) for argument in arguments))


def solution(mesh):
    return jax.shard_map(
        functools.partial(shards, mesh.shape["lat"], mesh.shape["lon"]),
        mesh=mesh,
        in_specs=(P("lat", "lon", None), P(), P(), P(), P(), P()),
        out_specs=P("lat", "lon", None),
        check_vma=False,
    )
```

```python
import functools
import math

import jax
import jax.numpy as jnp
from jax import lax
from jax.experimental import pallas as pl
from jax.experimental.pallas import tpu as pltpu
from jax.sharding import PartitionSpec as P

HEADS = 8
EPSILON = 1e-06
REACH = 3
TILE = 128
PACK = 4
SPANS = (2, 8, 4)
MESH = pl.DeviceIdType.MESH


def layer_norm(values):
    average = jnp.mean(values, axis=-1, keepdims=True)
    centered = values - average
    variance = jnp.mean(centered * centered, axis=-1, keepdims=True)
    return centered * lax.rsqrt(variance + EPSILON)


def dot(left, right):
    return jnp.dot(left, right, preferred_element_type=jnp.float32)


def dot_t(left, right):
    return lax.dot_general(left, right, (((1,), (1,)), ((), ())), preferred_element_type=jnp.float32)


def iotas(shape):
    return (lax.broadcasted_iota(jnp.int32, shape, 0), lax.broadcasted_iota(jnp.int32, shape, 1))


def far_first(step, members):
    return members // 2 + (step + 1) // 2 * (1 - 2 * (step % 2))


def wide(ref):
    return ref[...].astype(jnp.float32)


def kernel(
    lats,
    lons,
    field_hbm,
    taps_hbm,
    expand_hbm,
    reduce_hbm,
    lat_attn_hbm,
    lon_attn_hbm,
    out_ref,
    field,
    taps,
    expand,
    reduce,
    lat_attn,
    lon_attn,
    edge_first,
    edge_last,
    top,
    bottom,
    left,
    right,
    padded,
    sides,
    taps_wide,
    convolved,
    orders,
    block_packed,
    lat_out,
    lat_rows,
    lat_mix_out,
    lat_mix_rows,
    lon_out,
    lon_rows,
    lon_mix_out,
    lon_mix_rows,
    lon_queries,
    load_sems,
    halo_send,
    halo_recv,
    group_send,
    group_recv,
    ready_sems,
):
    rows, cols, channels = field.shape
    cells = rows * cols
    head_size = channels // HEADS
    per_tile = TILE // head_size
    lat, lon = lax.axis_index("lat"), lax.axis_index("lon")

    loads = [
        pltpu.make_async_copy(source, target, load_sems.at[index])
        for index, (source, target) in enumerate(
            (
                (field_hbm, field),
                (taps_hbm, taps),
                (lon_attn_hbm, lon_attn),
                (expand_hbm, expand),
                (reduce_hbm, reduce),
                (lat_attn_hbm, lat_attn),
            )
        )
    ]
    for load in loads:
        load.start()

    north, south = lax.rem(lat + lats - 1, lats), lax.rem(lat + 1, lats)
    west, east = lax.rem(lon + lons - 1, lons), lax.rem(lon + 1, lons)

    barrier = pltpu.get_barrier_semaphore()

    def greet(place):
        pl.semaphore_signal(barrier, inc=1, device_id=place, device_id_type=MESH)

    plane, line, column_place = lon // (SPANS[1] * SPANS[2]), lon // SPANS[2] % SPANS[1], lon % SPANS[2]

    planes = [plane * (SPANS[1] * SPANS[2]), (1 - plane) * (SPANS[1] * SPANS[2])]
    lines = [lax.rem(line + step, SPANS[1]) * SPANS[2] for step in range(SPANS[1])]
    places = [lax.rem(column_place + step, SPANS[2]) for step in range(SPANS[2])]

    def shifted(dz, dy, dx):
        return planes[dz] + lines[dy] + places[dx]

    for step in range(SPANS[1] - 1):
        greet((lat, shifted(0, far_first(step, SPANS[1]), 0)))
    for step in range(lats - 1):
        greet((lax.rem(lat + far_first(step, lats), lats), lon))
    for place in ((north, west), (north, east), (south, west), (south, east)):
        greet(place)
    greet((lat, west))
    greet((lat, east))
    greet((lat, shifted(1, 0, 0)))
    for step in range(1, SPANS[2]):
        greet((lat, shifted(0, 0, step)))

    loads[0].wait()
    edge_first[...] = field[:, :4]
    edge_last[...] = field[:, cols - 4 :]
    pl.semaphore_wait(barrier, lats - 1 + 4 + 2 + sum(SPANS) - len(SPANS))

    tail, head = pl.ds(rows - REACH, REACH), pl.ds(0, REACH)
    after, inner = pl.ds(rows + REACH, REACH), pl.ds(REACH, rows)
    halos = []
    for index, (source, target, place) in enumerate(
        (
            (edge_last, left.at[inner], (lat, east)),
            (edge_first, right.at[inner], (lat, west)),
            (field.at[tail], top, (south, lon)),
            (field.at[head], bottom, (north, lon)),
            (edge_last.at[tail], left.at[head], (south, east)),
            (edge_last.at[head], left.at[after], (north, east)),
            (edge_first.at[tail], right.at[head], (south, west)),
            (edge_first.at[head], right.at[after], (north, west)),
        )
    ):
        copy = pltpu.make_async_remote_copy(
            src_ref=source,
            dst_ref=target,
            send_sem=halo_send.at[index],
            recv_sem=halo_recv.at[index],
            device_id=place,
            device_id_type=MESH,
        )
        copy.start()
        halos.append(copy)

    def ready(index, place):
        pl.semaphore_signal(
            ready_sems.at[index], inc=1, device_id=place, device_id_type=MESH
        )

    for step in range(1, SPANS[2]):
        ready(0, (lat, shifted(0, 0, step)))

    def copy_to(phase, source, slot, place):
        return pltpu.make_async_remote_copy(
            src_ref=source,
            dst_ref=slot,
            send_sem=group_send.at[phase],
            recv_sem=group_recv.at[phase],
            device_id=place,
            device_id_type=MESH,
        )

    def all_of(phase, target, members):
        others = target.at[pl.ds(0, members - 1)]
        return copy_to(phase, others, others, (lat, lon))

    def exchange_lat(phase, source, target):
        for step in range(lats - 1):
            other = lax.rem(lat + far_first(step, lats), lats)
            copy_to(phase, source.at[other], target.at[lat], (other, lon)).start()
        target[lat] = source[lat]
        return all_of(phase, target, lats)

    loads[1].wait()
    taps_wide[...] = taps[...].astype(jnp.float32)
    padded[pl.ds(REACH, rows), :8] = jnp.zeros((rows, 8, channels), jnp.float32)
    padded[pl.ds(REACH, rows), 8 : 8 + cols] = wide(field)
    padded[pl.ds(REACH, rows), 8 + cols :] = jnp.zeros((rows, 8, channels), jnp.float32)
    sides[...] = jnp.zeros(sides.shape, jnp.float32)

    width = 2 * REACH + 1

    def tap_at(row_off, col_off, lanes):
        return taps_wide[row_off, col_off : col_off + 1, lanes]

    def add(sums, index, term):
        sums[index] = term if sums[index] is None else sums[index] + term

    def add_own(sums, view, col_off, lanes):
        for to_row in range(rows):
            for from_row in range(rows):
                row_off = from_row - to_row + REACH
                if 0 <= row_off < width:
                    add(sums, to_row, view[from_row] * tap_at(row_off, col_off, lanes))

    for half in range(channels // TILE):
        lanes = pl.ds(half * TILE, TILE)
        sums = [None] * rows
        for col_off in range(width):
            start = 8 - REACH + col_off
            add_own(sums, padded[pl.ds(REACH, rows), start : start + cols, lanes], col_off, lanes)
        for to_row in range(rows):
            convolved[to_row * cols : (to_row + 1) * cols, lanes] = sums[to_row]

    into, out_of = iotas((cells, cells))
    to_lon = (into // rows == out_of % cols) & (into % rows == out_of // cols)
    lon_packed = into // (rows * PACK) * PACK + into % PACK
    lat_packed = into // PACK % rows
    pack = out_of == lat_packed * cols + lon_packed
    pack_lon = out_of == lon_packed * rows + lat_packed
    lon_unpacked = out_of // (rows * PACK) * PACK + out_of % PACK
    unpack = into == (out_of // PACK % rows) * cols + lon_unpacked
    for index, chosen in enumerate((to_lon, pack, pack_lon, unpack)):
        orders[index] = chosen.astype(jnp.float32).astype(jnp.bfloat16)
    loads[2].wait()
    loads[3].wait()
    loads[4].wait()
    loads[5].wait()

    for copy in halos:
        copy.wait_recv()
    pl.semaphore_wait(ready_sems.at[0], SPANS[2] - 1)
    ready(1, (lat, shifted(1, 0, 0)))
    not_first = (lat > 0).astype(jnp.float32)
    not_last = (lat < lats - 1).astype(jnp.float32)
    padded[pl.ds(0, REACH), 8 : 8 + cols] = wide(top) * not_first
    padded[pl.ds(rows + REACH, REACH), 8 : 8 + cols] = wide(bottom) * not_last
    for side, start in ((left, 4), (right, 8 + cols)):
        values = wide(side)
        padded[pl.ds(0, REACH), start : start + 4] = values[:REACH] * not_first
        sides[:, start : start + 4] = values[REACH : REACH + rows]
        padded[pl.ds(rows + REACH, REACH), start : start + 4] = values[REACH + rows :] * not_last

    for half in range(channels // TILE):
        lanes = pl.ds(half * TILE, TILE)
        sums = [convolved[row * cols : (row + 1) * cols, lanes] for row in range(rows)]
        for col_off in range(width):
            start = 8 - REACH + col_off
            before = padded[pl.ds(0, REACH), start : start + cols, lanes]
            behind = padded[pl.ds(rows + REACH, REACH), start : start + cols, lanes]
            for from_row in range(REACH):
                for to_row in range(from_row + 1):
                    tap = tap_at(from_row - to_row, col_off, lanes)
                    add(sums, to_row, before[from_row] * tap)
                for to_row in range(rows - REACH + from_row, rows):
                    tap = tap_at(rows + REACH + from_row - to_row, col_off, lanes)
                    add(sums, to_row, behind[from_row] * tap)
        ends = []
        for first, offsets in ((0, range(REACH)), (cols - 8, range(REACH + 1, width))):
            strips = [None] * rows
            for col_off in offsets:
                start = 8 - REACH + col_off + first
                add_own(strips, sides[:, start : start + 8, lanes], col_off, lanes)
            ends.append(strips)
        for to_row in range(rows):
            strip = jnp.concatenate([ends[0][to_row], ends[1][to_row]], axis=0)
            convolved[to_row * cols : (to_row + 1) * cols, lanes] = sums[to_row] + strip

    normed = layer_norm(convolved[...]).astype(jnp.bfloat16)
    hidden = dot(normed, expand[...])
    hidden = 0.5 * hidden * (1.0 + lax.erf(hidden * (0.5**0.5)))
    own = field[...].astype(jnp.float32).reshape(cells, channels)
    block_one = (own + dot(hidden.astype(jnp.bfloat16), reduce[...])).astype(jnp.bfloat16)
    lat_in = layer_norm(block_one.astype(jnp.float32)).astype(jnp.bfloat16)

    by_lon = dot(orders[0], lat_in).astype(jnp.bfloat16)
    block_rows = cells // lats
    lat_out[...] = by_lon.reshape(lats, block_rows, channels)
    pending = exchange_lat(0, lat_out, lat_rows)
    block_packed[...] = dot(orders[1], block_one)
    pending.wait_recv()

    column = lat_rows[...].reshape(cells, channels)
    scale = head_size ** (-0.5) * math.log2(math.e)
    queries = (dot(column, lat_attn[0]) * scale).astype(jnp.bfloat16)
    keys = dot(column, lat_attn[1]).astype(jnp.bfloat16)
    values = dot(column, lat_attn[2]).astype(jnp.bfloat16)
    lane = lax.broadcasted_iota(jnp.int32, (cells, channels), 1)
    query_row, key_row = iotas((cells, cells))
    same = query_row // rows % (block_rows // rows) == key_row // rows % (block_rows // rows)
    mixed = jnp.zeros((cells, channels), jnp.float32)
    for head_index in range(HEADS):
        mine = lane // head_size == head_index
        scores = dot_t(queries, jnp.where(mine, keys, jnp.zeros_like(keys)))
        scores = jnp.where(same, scores, -1e30)
        probs = jnp.exp2(scores - jnp.max(scores, axis=-1, keepdims=True))
        probs = probs / jnp.sum(probs, axis=-1, keepdims=True)
        mixed = mixed + dot(
            probs.astype(jnp.bfloat16), jnp.where(mine, values, jnp.zeros_like(values))
        )
    lat_mix_out[...] = mixed.astype(jnp.bfloat16).reshape(lats, block_rows, channels)
    pending.wait_send()
    pending = exchange_lat(1, lat_mix_out, lat_mix_rows)
    pending.wait_recv()

    lat_mix = dot(orders[2], lat_mix_rows[...].reshape(cells, channels)).astype(jnp.bfloat16)
    block_two = (block_packed[...] + dot(lat_mix, lat_attn[3])).astype(jnp.bfloat16)
    block_packed[...] = block_two.astype(jnp.float32)
    lon_in = layer_norm(block_two.astype(jnp.float32)).astype(jnp.bfloat16)
    part = rows * PACK
    spot = lax.broadcasted_iota(jnp.int32, (part, TILE), 1) // head_size
    for kind in range(3):
        projected = dot(lon_in, lon_attn[kind])
        if kind == 0:
            projected = projected * scale
        projected = projected.astype(jnp.bfloat16)
        for head_index in range(HEADS):
            tile, spot_from = head_index // per_tile * TILE, head_index % per_tile
            block = None
            for spot_to in range(per_tile):
                piece = projected[spot_to * part : (spot_to + 1) * part, tile : tile + TILE]
                if spot_to != spot_from:
                    piece = pltpu.roll(piece, (spot_to - spot_from) * head_size % TILE, 1)
                block = piece if block is None else jnp.where(spot == spot_to, piece, block)
            for row_index in range(rows):
                lon_out[row_index * HEADS + head_index, kind] = block[
                    row_index * PACK : (row_index + 1) * PACK
                ]
    pending.wait_send()
    pl.semaphore_wait(ready_sems.at[1], 1)

    for step in range(lons - 1):
        other = shifted(
            1 - step % 2,
            far_first(step // (SPANS[0] * SPANS[2]), SPANS[1]),
            far_first(step // SPANS[0] % SPANS[2], SPANS[2]),
        )
        copy_to(2, lon_out.at[other], lon_rows.at[lon], (lat, other)).start()
    lon_rows[lon] = lon_out[lon]
    pending = all_of(2, lon_rows, lons)
    pending.wait_recv()

    length = lons * cols
    packed_rows = length // per_tile
    source, target = iotas((TILE, per_tile * TILE))
    spread = target % TILE < head_size
    spread = spread & (source == target // TILE * head_size + target % TILE)
    spread = spread.astype(jnp.float32).astype(jnp.bfloat16)

    def apart(packed):
        return dot(packed, spread).astype(jnp.bfloat16)

    def stacked(parts):
        return jnp.concatenate(
            [parts[:, index * TILE : (index + 1) * TILE] for index in range(per_tile)], axis=0
        )

    keys = stacked(apart(lon_rows[:, 1].reshape(packed_rows, TILE)))
    values = stacked(apart(lon_rows[:, 2].reshape(packed_rows, TILE)))
    values = jnp.concatenate([values, jnp.ones((length, TILE), jnp.bfloat16)], axis=1)
    pending.wait_send()
    spread_queries = apart(lon_rows[:, 0].reshape(packed_rows, TILE))
    for index in range(per_tile):
        lon_queries[index] = spread_queries[:, index * TILE : (index + 1) * TILE]
    per_step = 2
    run = SPANS[2] * PACK
    def prepare(step):
        offsets = [
            (dz, far_first(step + index, SPANS[1])) for index in range(per_step) for dz in (1, 0)
        ]
        firsts = [planes[dz] + lines[dy] for dz, dy in offsets]
        spots = [pl.ds(pl.multiple_of(first * PACK, run), run) for first in firsts]
        queries = jnp.concatenate(
            [lon_queries[index, rows_of] for index in range(per_tile) for rows_of in spots], axis=0
        )
        scores = dot_t(queries, keys)
        return scores, firsts, offsets

    upcoming = prepare(0)
    for step in range(0, SPANS[1], per_step):
        scores, firsts, offsets = upcoming
        if step + per_step < SPANS[1]:
            upcoming = prepare(step + per_step)
        probs = jnp.exp2(scores - jnp.max(scores, axis=-1, keepdims=True))
        mixed = dot(probs.astype(jnp.bfloat16), values)
        mixed = mixed[:, :TILE] / mixed[:, TILE:]
        chunk = run * len(offsets)
        block = mixed[:chunk]
        for index in range(1, per_tile):
            piece = mixed[index * chunk : (index + 1) * chunk]
            block = block + pltpu.roll(piece, index * head_size, 1)
        block = block.astype(jnp.bfloat16)
        for index, (first, (dz, dy)) in enumerate(zip(firsts, offsets)):
            lon_mix_out[pl.ds(first, SPANS[2])] = block[index * run : (index + 1) * run].reshape(
                SPANS[2], PACK, TILE
            )
        for dz, dy in offsets:
            for dx in (2, 1, 3, 0):
                if (dz, dy, dx) != (0, 0, 0):
                    other = shifted(dz, dy, dx)
                    copy_to(3, lon_mix_out.at[other], lon_mix_rows.at[lon], (lat, other)).start()
    lon_mix_rows[lon] = lon_mix_out[lon]
    pending = all_of(3, lon_mix_rows, lons)
    pending.wait_recv()

    result = block_packed[...]
    for tile in range(channels // TILE):
        heads = [
            jnp.concatenate(
                [
                    lon_mix_rows[row_index * HEADS + head_index]
                    for row_index in range(rows)
                ],
                axis=0,
            )
            for head_index in range(per_tile * tile, per_tile * (tile + 1))
        ]
        parts = []
        for spot_from in range(per_tile):
            block = None
            for spot_to in range(per_tile):
                piece = heads[spot_to]
                if spot_to != spot_from:
                    piece = pltpu.roll(piece, (spot_to - spot_from) * head_size % TILE, 1)
                block = piece if block is None else jnp.where(spot == spot_to, piece, block)
            parts.append(block)
        mixture = jnp.concatenate(parts, axis=0)
        result = result + dot(mixture, lon_attn[3, tile * TILE : (tile + 1) * TILE])
    result = dot(orders[3], result.astype(jnp.bfloat16)).astype(jnp.bfloat16)
    out_ref[...] = result.reshape(rows, cols, channels)
    pending.wait_send()
    for copy in halos:
        copy.wait_send()


def shards(lats, lons, field, dw_weight, w_expand, w_reduce, lat_attn, lon_attn):
    rows, cols, channels = field.shape
    cells = rows * cols
    bf16, f32 = jnp.bfloat16, jnp.float32
    arguments = (field, dw_weight, w_expand, w_reduce, lat_attn, lon_attn)
    vmem = pltpu.VMEM
    edge = vmem((rows, 4, channels), bf16)
    strip = vmem((REACH, cols, channels), bf16)
    side = vmem((rows + 2 * REACH, 4, channels), bf16)
    column = vmem((lats, cells // lats, channels), bf16)
    mix = vmem((lons, PACK, TILE), bf16)
    return pl.pallas_call(
        functools.partial(kernel, lats, lons),
        out_shape=jax.ShapeDtypeStruct(field.shape, field.dtype),
        in_specs=[pl.BlockSpec(memory_space=pltpu.HBM)] * len(arguments),
        out_specs=pl.BlockSpec(memory_space=pltpu.VMEM),
        scratch_shapes=[
            *(vmem(argument.shape, argument.dtype) for argument in arguments),
            edge,
            edge,
            strip,
            strip,
            side,
            side,
            vmem((rows + 2 * REACH, cols + 16, channels), f32),
            vmem((rows, cols + 16, channels), f32),
            vmem(dw_weight.shape, f32),
            vmem((cells, channels), f32),
            vmem((4, cells, cells), bf16),
            vmem((cells, channels), f32),
            column,
            column,
            column,
            column,
            vmem((lons, 3, PACK, TILE), bf16),
            vmem((lons, 3, PACK, TILE), bf16),
            mix,
            mix,
            vmem((TILE * HEADS // channels, lons * PACK, TILE), bf16),
            pltpu.SemaphoreType.DMA((len(arguments),)),
            pltpu.SemaphoreType.DMA((8,)),
            pltpu.SemaphoreType.DMA((8,)),
            pltpu.SemaphoreType.DMA((4,)),
            pltpu.SemaphoreType.DMA((4,)),
            pltpu.SemaphoreType.REGULAR((2,)),
        ],
        compiler_params=pltpu.CompilerParams(
            collective_id=0, has_side_effects=True, vmem_limit_bytes=48 << 20
        ),
        name="block",
    )(*(pltpu.with_memory_space_constraint(argument, pltpu.HBM) for argument in arguments))


def solution(mesh):
    return jax.shard_map(
        functools.partial(shards, mesh.shape["lat"], mesh.shape["lon"]),
        mesh=mesh,
        in_specs=(P("lat", "lon", None), P(), P(), P(), P(), P()),
        out_specs=P("lat", "lon", None),
        check_vma=False,
    )
```

```python
import functools
import math

import jax
import jax.numpy as jnp
from jax import lax
from jax.experimental import pallas as pl
from jax.experimental.pallas import tpu as pltpu
from jax.sharding import PartitionSpec as P

HEADS = 8
EPSILON = 1e-06
REACH = 3
TILE = 128
PACK = 4
SPANS = (2, 8, 4)
MESH = pl.DeviceIdType.MESH


def layer_norm(values):
    average = jnp.mean(values, axis=-1, keepdims=True)
    centered = values - average
    variance = jnp.mean(centered * centered, axis=-1, keepdims=True)
    return centered * lax.rsqrt(variance + EPSILON)


def dot(left, right):
    return jnp.dot(left, right, preferred_element_type=jnp.float32)


def dot_t(left, right):
    return lax.dot_general(left, right, (((1,), (1,)), ((), ())), preferred_element_type=jnp.float32)


def iotas(shape):
    return (lax.broadcasted_iota(jnp.int32, shape, 0), lax.broadcasted_iota(jnp.int32, shape, 1))


def far_first(step, members):
    return members // 2 + (step + 1) // 2 * (1 - 2 * (step % 2))


def wide(ref):
    return ref[...].astype(jnp.float32)


def kernel(
    lats,
    lons,
    field_hbm,
    taps_hbm,
    expand_hbm,
    reduce_hbm,
    lat_attn_hbm,
    lon_attn_hbm,
    out_ref,
    field,
    taps,
    expand,
    reduce,
    lat_attn,
    lon_attn,
    edge_first,
    edge_last,
    top,
    bottom,
    left,
    right,
    padded,
    sides,
    taps_wide,
    convolved,
    orders,
    block_packed,
    lat_out,
    lat_rows,
    lat_mix_out,
    lat_mix_rows,
    lon_out,
    lon_rows,
    lon_mix_out,
    lon_mix_rows,
    lon_queries,
    load_sems,
    halo_send,
    halo_recv,
    group_send,
    group_recv,
    ready_sems,
):
    rows, cols, channels = field.shape
    cells = rows * cols
    head_size = channels // HEADS
    per_tile = TILE // head_size
    lat, lon = lax.axis_index("lat"), lax.axis_index("lon")

    loads = [
        pltpu.make_async_copy(source, target, load_sems.at[index])
        for index, (source, target) in enumerate(
            (
                (field_hbm, field),
                (taps_hbm, taps),
                (lon_attn_hbm, lon_attn),
                (expand_hbm, expand),
                (reduce_hbm, reduce),
                (lat_attn_hbm, lat_attn),
            )
        )
    ]
    for load in loads:
        load.start()

    north, south = lax.rem(lat + lats - 1, lats), lax.rem(lat + 1, lats)
    west, east = lax.rem(lon + lons - 1, lons), lax.rem(lon + 1, lons)

    barrier = pltpu.get_barrier_semaphore()

    def greet(place):
        pl.semaphore_signal(barrier, inc=1, device_id=place, device_id_type=MESH)

    plane, line, column_place = lon // (SPANS[1] * SPANS[2]), lon // SPANS[2] % SPANS[1], lon % SPANS[2]

    planes = [plane * (SPANS[1] * SPANS[2]), (1 - plane) * (SPANS[1] * SPANS[2])]
    lines = [lax.rem(line + step, SPANS[1]) * SPANS[2] for step in range(SPANS[1])]
    places = [lax.rem(column_place + step, SPANS[2]) for step in range(SPANS[2])]

    def shifted(dz, dy, dx):
        return planes[dz] + lines[dy] + places[dx]

    for step in range(SPANS[1] - 1):
        greet((lat, shifted(0, far_first(step, SPANS[1]), 0)))
    for step in range(lats - 1):
        greet((lax.rem(lat + far_first(step, lats), lats), lon))
    for place in ((north, west), (north, east), (south, west), (south, east)):
        greet(place)
    greet((lat, west))
    greet((lat, east))
    greet((lat, shifted(1, 0, 0)))
    for step in range(1, SPANS[2]):
        greet((lat, shifted(0, 0, step)))

    loads[0].wait()
    edge_first[...] = field[:, :4]
    edge_last[...] = field[:, cols - 4 :]
    pl.semaphore_wait(barrier, lats - 1 + 4 + 2 + sum(SPANS) - len(SPANS))

    tail, head = pl.ds(rows - REACH, REACH), pl.ds(0, REACH)
    after, inner = pl.ds(rows + REACH, REACH), pl.ds(REACH, rows)
    halos = []
    for index, (source, target, place) in enumerate(
        (
            (edge_last, left.at[inner], (lat, east)),
            (edge_first, right.at[inner], (lat, west)),
            (field.at[tail], top, (south, lon)),
            (field.at[head], bottom, (north, lon)),
            (edge_last.at[tail], left.at[head], (south, east)),
            (edge_last.at[head], left.at[after], (north, east)),
            (edge_first.at[tail], right.at[head], (south, west)),
            (edge_first.at[head], right.at[after], (north, west)),
        )
    ):
        copy = pltpu.make_async_remote_copy(
            src_ref=source,
            dst_ref=target,
            send_sem=halo_send.at[index],
            recv_sem=halo_recv.at[index],
            device_id=place,
            device_id_type=MESH,
        )
        copy.start()
        halos.append(copy)

    def ready(index, place):
        pl.semaphore_signal(
            ready_sems.at[index], inc=1, device_id=place, device_id_type=MESH
        )

    for step in range(1, SPANS[2]):
        ready(0, (lat, shifted(0, 0, step)))

    def copy_to(phase, source, slot, place):
        return pltpu.make_async_remote_copy(
            src_ref=source,
            dst_ref=slot,
            send_sem=group_send.at[phase],
            recv_sem=group_recv.at[phase],
            device_id=place,
            device_id_type=MESH,
        )

    def all_of(phase, target, members):
        others = target.at[pl.ds(0, members - 1)]
        return copy_to(phase, others, others, (lat, lon))

    def exchange_lat(phase, source, target):
        for step in range(lats - 1):
            other = lax.rem(lat + far_first(step, lats), lats)
            copy_to(phase, source.at[other], target.at[lat], (other, lon)).start()
        target[lat] = source[lat]
        return all_of(phase, target, lats)

    loads[1].wait()
    taps_wide[...] = taps[...].astype(jnp.float32)
    padded[pl.ds(REACH, rows), :8] = jnp.zeros((rows, 8, channels), jnp.float32)
    padded[pl.ds(REACH, rows), 8 : 8 + cols] = wide(field)
    padded[pl.ds(REACH, rows), 8 + cols :] = jnp.zeros((rows, 8, channels), jnp.float32)
    sides[...] = jnp.zeros(sides.shape, jnp.float32)

    width = 2 * REACH + 1

    def tap_at(row_off, col_off, lanes):
        return taps_wide[row_off, col_off : col_off + 1, lanes]

    def add(sums, index, term):
        sums[index] = term if sums[index] is None else sums[index] + term

    def add_own(sums, view, col_off, lanes):
        for to_row in range(rows):
            for from_row in range(rows):
                row_off = from_row - to_row + REACH
                if 0 <= row_off < width:
                    add(sums, to_row, view[from_row] * tap_at(row_off, col_off, lanes))

    for half in range(channels // TILE):
        lanes = pl.ds(half * TILE, TILE)
        sums = [None] * rows
        for col_off in range(width):
            start = 8 - REACH + col_off
            add_own(sums, padded[pl.ds(REACH, rows), start : start + cols, lanes], col_off, lanes)
        for to_row in range(rows):
            convolved[to_row * cols : (to_row + 1) * cols, lanes] = sums[to_row]

    into, out_of = iotas((cells, cells))
    to_lon = (into // rows == out_of % cols) & (into % rows == out_of // cols)
    lon_packed = into // (rows * PACK) * PACK + into % PACK
    lat_packed = into // PACK % rows
    pack = out_of == lat_packed * cols + lon_packed
    pack_lon = out_of == lon_packed * rows + lat_packed
    lon_unpacked = out_of // (rows * PACK) * PACK + out_of % PACK
    unpack = into == (out_of // PACK % rows) * cols + lon_unpacked
    for index, chosen in enumerate((to_lon, pack, pack_lon, unpack)):
        orders[index] = chosen.astype(jnp.float32).astype(jnp.bfloat16)
    loads[2].wait()
    loads[3].wait()
    loads[4].wait()
    loads[5].wait()

    for copy in halos:
        copy.wait_recv()
    pl.semaphore_wait(ready_sems.at[0], SPANS[2] - 1)
    ready(1, (lat, shifted(1, 0, 0)))
    not_first = (lat > 0).astype(jnp.float32)
    not_last = (lat < lats - 1).astype(jnp.float32)
    padded[pl.ds(0, REACH), 8 : 8 + cols] = wide(top) * not_first
    padded[pl.ds(rows + REACH, REACH), 8 : 8 + cols] = wide(bottom) * not_last
    for side, start in ((left, 4), (right, 8 + cols)):
        values = wide(side)
        padded[pl.ds(0, REACH), start : start + 4] = values[:REACH] * not_first
        sides[:, start : start + 4] = values[REACH : REACH + rows]
        padded[pl.ds(rows + REACH, REACH), start : start + 4] = values[REACH + rows :] * not_last

    for half in range(channels // TILE):
        lanes = pl.ds(half * TILE, TILE)
        sums = [convolved[row * cols : (row + 1) * cols, lanes] for row in range(rows)]
        for col_off in range(width):
            start = 8 - REACH + col_off
            before = padded[pl.ds(0, REACH), start : start + cols, lanes]
            behind = padded[pl.ds(rows + REACH, REACH), start : start + cols, lanes]
            for from_row in range(REACH):
                for to_row in range(from_row + 1):
                    tap = tap_at(from_row - to_row, col_off, lanes)
                    add(sums, to_row, before[from_row] * tap)
                for to_row in range(rows - REACH + from_row, rows):
                    tap = tap_at(rows + REACH + from_row - to_row, col_off, lanes)
                    add(sums, to_row, behind[from_row] * tap)
        ends = []
        for first, offsets in ((0, range(REACH)), (cols - 8, range(REACH + 1, width))):
            strips = [None] * rows
            for col_off in offsets:
                start = 8 - REACH + col_off + first
                add_own(strips, sides[:, start : start + 8, lanes], col_off, lanes)
            ends.append(strips)
        for to_row in range(rows):
            strip = jnp.concatenate([ends[0][to_row], ends[1][to_row]], axis=0)
            convolved[to_row * cols : (to_row + 1) * cols, lanes] = sums[to_row] + strip

    normed = layer_norm(convolved[...]).astype(jnp.bfloat16)
    hidden = dot(normed, expand[...])
    hidden = 0.5 * hidden * (1.0 + lax.erf(hidden * (0.5**0.5)))
    own = field[...].astype(jnp.float32).reshape(cells, channels)
    block_one = (own + dot(hidden.astype(jnp.bfloat16), reduce[...])).astype(jnp.bfloat16)
    lat_in = layer_norm(block_one.astype(jnp.float32)).astype(jnp.bfloat16)

    by_lon = dot(orders[0], lat_in).astype(jnp.bfloat16)
    block_rows = cells // lats
    lat_out[...] = by_lon.reshape(lats, block_rows, channels)
    pending = exchange_lat(0, lat_out, lat_rows)
    block_packed[...] = dot(orders[1], block_one)
    pending.wait_recv()

    column = lat_rows[...].reshape(cells, channels)
    scale = head_size ** (-0.5) * math.log2(math.e)
    queries = (dot(column, lat_attn[0]) * scale).astype(jnp.bfloat16)
    keys = dot(column, lat_attn[1]).astype(jnp.bfloat16)
    values = dot(column, lat_attn[2]).astype(jnp.bfloat16)
    lane = lax.broadcasted_iota(jnp.int32, (cells, channels), 1)
    query_row, key_row = iotas((cells, cells))
    same = query_row // rows % (block_rows // rows) == key_row // rows % (block_rows // rows)

    def by_head(array):
        zeros = jnp.zeros_like(array)
        return jnp.concatenate(
            [jnp.where(lane // head_size == index, array, zeros) for index in range(HEADS)], axis=0
        )

    all_scores = dot_t(queries, by_head(keys))
    all_probs = []
    for head_index in range(HEADS):
        scores = all_scores[:, head_index * cells : (head_index + 1) * cells]
        scores = jnp.where(same, scores, -3e38)
        probs = jnp.exp2(scores - jnp.max(scores, axis=-1, keepdims=True))
        probs = probs * (1.0 / jnp.sum(probs, axis=-1, keepdims=True))
        all_probs.append(probs.astype(jnp.bfloat16))
    mixed = dot(jnp.concatenate(all_probs, axis=1), by_head(values))
    lat_mix_out[...] = mixed.astype(jnp.bfloat16).reshape(lats, block_rows, channels)
    pending.wait_send()
    pending = exchange_lat(1, lat_mix_out, lat_mix_rows)
    pending.wait_recv()

    lat_mix = dot(orders[2], lat_mix_rows[...].reshape(cells, channels)).astype(jnp.bfloat16)
    block_two = (block_packed[...] + dot(lat_mix, lat_attn[3])).astype(jnp.bfloat16)
    block_packed[...] = block_two.astype(jnp.float32)
    lon_in = layer_norm(block_two.astype(jnp.float32)).astype(jnp.bfloat16)
    part = rows * PACK
    spot = lax.broadcasted_iota(jnp.int32, (part, TILE), 1) // head_size
    for kind in range(3):
        projected = dot(lon_in, lon_attn[kind])
        if kind == 0:
            projected = projected * scale
        projected = projected.astype(jnp.bfloat16)
        for head_index in range(HEADS):
            tile, spot_from = head_index // per_tile * TILE, head_index % per_tile
            block = None
            for spot_to in range(per_tile):
                piece = projected[spot_to * part : (spot_to + 1) * part, tile : tile + TILE]
                if spot_to != spot_from:
                    piece = pltpu.roll(piece, (spot_to - spot_from) * head_size % TILE, 1)
                block = piece if block is None else jnp.where(spot == spot_to, piece, block)
            for row_index in range(rows):
                lon_out[row_index * HEADS + head_index, kind] = block[
                    row_index * PACK : (row_index + 1) * PACK
                ]
    pending.wait_send()
    pl.semaphore_wait(ready_sems.at[1], 1)

    for step in range(lons - 1):
        other = shifted(
            1 - step % 2,
            far_first(step // (SPANS[0] * SPANS[2]), SPANS[1]),
            far_first(step // SPANS[0] % SPANS[2], SPANS[2]),
        )
        copy_to(2, lon_out.at[other], lon_rows.at[lon], (lat, other)).start()
    lon_rows[lon] = lon_out[lon]
    pending = all_of(2, lon_rows, lons)
    pending.wait_recv()

    length = lons * cols
    packed_rows = length // per_tile
    source, target = iotas((TILE, per_tile * TILE))
    spread = target % TILE < head_size
    spread = spread & (source == target // TILE * head_size + target % TILE)
    spread = spread.astype(jnp.float32).astype(jnp.bfloat16)

    def apart(packed):
        return dot(packed, spread).astype(jnp.bfloat16)

    def stacked(parts):
        return jnp.concatenate(
            [parts[:, index * TILE : (index + 1) * TILE] for index in range(per_tile)], axis=0
        )

    keys = stacked(apart(lon_rows[:, 1].reshape(packed_rows, TILE)))
    values = stacked(apart(lon_rows[:, 2].reshape(packed_rows, TILE)))
    values = jnp.concatenate([values, jnp.ones((length, TILE), jnp.bfloat16)], axis=1)
    pending.wait_send()
    spread_queries = apart(lon_rows[:, 0].reshape(packed_rows, TILE))
    for index in range(per_tile):
        lon_queries[index] = spread_queries[:, index * TILE : (index + 1) * TILE]
    per_step = 2
    run = SPANS[2] * PACK
    def prepare(step):
        offsets = [
            (dz, far_first(step + index, SPANS[1])) for index in range(per_step) for dz in (1, 0)
        ]
        firsts = [planes[dz] + lines[dy] for dz, dy in offsets]
        spots = [pl.ds(pl.multiple_of(first * PACK, run), run) for first in firsts]
        queries = jnp.concatenate(
            [lon_queries[index, rows_of] for index in range(per_tile) for rows_of in spots], axis=0
        )
        scores = dot_t(queries, keys)
        return scores, firsts, offsets

    upcoming = prepare(0)
    for step in range(0, SPANS[1], per_step):
        scores, firsts, offsets = upcoming
        if step + per_step < SPANS[1]:
            upcoming = prepare(step + per_step)
        probs = jnp.exp2(scores - jnp.max(scores, axis=-1, keepdims=True))
        mixed = dot(probs.astype(jnp.bfloat16), values)
        mixed = mixed[:, :TILE] / mixed[:, TILE:]
        chunk = run * len(offsets)
        block = mixed[:chunk]
        for index in range(1, per_tile):
            piece = mixed[index * chunk : (index + 1) * chunk]
            block = block + pltpu.roll(piece, index * head_size, 1)
        block = block.astype(jnp.bfloat16)
        for index, (first, (dz, dy)) in enumerate(zip(firsts, offsets)):
            lon_mix_out[pl.ds(first, SPANS[2])] = block[index * run : (index + 1) * run].reshape(
                SPANS[2], PACK, TILE
            )
        for dz, dy in offsets:
            for dx in (2, 1, 3, 0):
                if (dz, dy, dx) != (0, 0, 0):
                    other = shifted(dz, dy, dx)
                    copy_to(3, lon_mix_out.at[other], lon_mix_rows.at[lon], (lat, other)).start()
    lon_mix_rows[lon] = lon_mix_out[lon]
    pending = all_of(3, lon_mix_rows, lons)
    pending.wait_recv()

    result = block_packed[...]
    for tile in range(channels // TILE):
        heads = [
            jnp.concatenate(
                [
                    lon_mix_rows[row_index * HEADS + head_index]
                    for row_index in range(rows)
                ],
                axis=0,
            )
            for head_index in range(per_tile * tile, per_tile * (tile + 1))
        ]
        parts = []
        for spot_from in range(per_tile):
            block = None
            for spot_to in range(per_tile):
                piece = heads[spot_to]
                if spot_to != spot_from:
                    piece = pltpu.roll(piece, (spot_to - spot_from) * head_size % TILE, 1)
                block = piece if block is None else jnp.where(spot == spot_to, piece, block)
            parts.append(block)
        mixture = jnp.concatenate(parts, axis=0)
        result = result + dot(mixture, lon_attn[3, tile * TILE : (tile + 1) * TILE])
    result = result.astype(jnp.bfloat16)
    for index in range(cols // PACK):
        for row_index in range(rows):
            start = index * part + row_index * PACK
            out_ref[row_index, index * PACK : (index + 1) * PACK] = result[start : start + PACK]
    pending.wait_send()
    for copy in halos:
        copy.wait_send()


def shards(lats, lons, field, dw_weight, w_expand, w_reduce, lat_attn, lon_attn):
    rows, cols, channels = field.shape
    cells = rows * cols
    bf16, f32 = jnp.bfloat16, jnp.float32
    arguments = (field, dw_weight, w_expand, w_reduce, lat_attn, lon_attn)
    vmem = pltpu.VMEM
    edge = vmem((rows, 4, channels), bf16)
    strip = vmem((REACH, cols, channels), bf16)
    side = vmem((rows + 2 * REACH, 4, channels), bf16)
    column = vmem((lats, cells // lats, channels), bf16)
    mix = vmem((lons, PACK, TILE), bf16)
    return pl.pallas_call(
        functools.partial(kernel, lats, lons),
        out_shape=jax.ShapeDtypeStruct(field.shape, field.dtype),
        in_specs=[pl.BlockSpec(memory_space=pltpu.HBM)] * len(arguments),
        out_specs=pl.BlockSpec(memory_space=pltpu.VMEM),
        scratch_shapes=[
            *(vmem(argument.shape, argument.dtype) for argument in arguments),
            edge,
            edge,
            strip,
            strip,
            side,
            side,
            vmem((rows + 2 * REACH, cols + 16, channels), f32),
            vmem((rows, cols + 16, channels), f32),
            vmem(dw_weight.shape, f32),
            vmem((cells, channels), f32),
            vmem((4, cells, cells), bf16),
            vmem((cells, channels), f32),
            column,
            column,
            column,
            column,
            vmem((lons, 3, PACK, TILE), bf16),
            vmem((lons, 3, PACK, TILE), bf16),
            mix,
            mix,
            vmem((TILE * HEADS // channels, lons * PACK, TILE), bf16),
            pltpu.SemaphoreType.DMA((len(arguments),)),
            pltpu.SemaphoreType.DMA((8,)),
            pltpu.SemaphoreType.DMA((8,)),
            pltpu.SemaphoreType.DMA((4,)),
            pltpu.SemaphoreType.DMA((4,)),
            pltpu.SemaphoreType.REGULAR((2,)),
        ],
        compiler_params=pltpu.CompilerParams(
            collective_id=0, has_side_effects=True, vmem_limit_bytes=48 << 20
        ),
        name="block",
    )(*(pltpu.with_memory_space_constraint(argument, pltpu.HBM) for argument in arguments))


def solution(mesh):
    return jax.shard_map(
        functools.partial(shards, mesh.shape["lat"], mesh.shape["lon"]),
        mesh=mesh,
        in_specs=(P("lat", "lon", None), P(), P(), P(), P(), P()),
        out_specs=P("lat", "lon", None),
        check_vma=False,
    )
```

```python
import functools
import math

import jax
import jax.numpy as jnp
from jax import lax
from jax.experimental import pallas as pl
from jax.experimental.pallas import tpu as pltpu
from jax.sharding import PartitionSpec as P

HEADS = 8
EPSILON = 1e-06
REACH = 3
TILE = 128
PACK = 4
SPANS = (2, 8, 4)
MESH = pl.DeviceIdType.MESH


def layer_norm(values):
    average = jnp.mean(values, axis=-1, keepdims=True)
    centered = values - average
    variance = jnp.mean(centered * centered, axis=-1, keepdims=True)
    return centered * lax.rsqrt(variance + EPSILON)


def dot(left, right):
    return jnp.dot(left, right, preferred_element_type=jnp.float32)


def dot_t(left, right):
    return lax.dot_general(left, right, (((1,), (1,)), ((), ())), preferred_element_type=jnp.float32)


def iotas(shape):
    return (lax.broadcasted_iota(jnp.int32, shape, 0), lax.broadcasted_iota(jnp.int32, shape, 1))


def far_first(step, members):
    return members // 2 + (step + 1) // 2 * (1 - 2 * (step % 2))


def wide(ref):
    return ref[...].astype(jnp.float32)


def kernel(
    lats,
    lons,
    field_hbm,
    taps_hbm,
    expand_hbm,
    reduce_hbm,
    lat_attn_hbm,
    lon_attn_hbm,
    out_ref,
    field,
    taps,
    expand,
    reduce,
    lat_attn,
    lon_attn,
    edge_first,
    edge_last,
    top,
    bottom,
    left,
    right,
    padded,
    sides,
    taps_wide,
    convolved,
    orders,
    block_packed,
    lat_out,
    lat_rows,
    lat_mix_out,
    lat_mix_rows,
    lon_out,
    lon_rows,
    lon_mix_out,
    lon_mix_rows,
    lon_queries,
    spreading,
    load_sems,
    halo_send,
    halo_recv,
    group_send,
    group_recv,
    ready_sems,
):
    rows, cols, channels = field.shape
    cells = rows * cols
    head_size = channels // HEADS
    per_tile = TILE // head_size
    lat, lon = lax.axis_index("lat"), lax.axis_index("lon")

    loads = [
        pltpu.make_async_copy(source, target, load_sems.at[index])
        for index, (source, target) in enumerate(
            (
                (field_hbm, field),
                (taps_hbm, taps),
                (lon_attn_hbm, lon_attn),
                (expand_hbm, expand),
                (reduce_hbm, reduce),
                (lat_attn_hbm, lat_attn),
            )
        )
    ]
    for load in loads:
        load.start()

    north, south = lax.rem(lat + lats - 1, lats), lax.rem(lat + 1, lats)
    west, east = lax.rem(lon + lons - 1, lons), lax.rem(lon + 1, lons)

    barrier = pltpu.get_barrier_semaphore()

    def greet(place):
        pl.semaphore_signal(barrier, inc=1, device_id=place, device_id_type=MESH)

    plane, line, column_place = lon // (SPANS[1] * SPANS[2]), lon // SPANS[2] % SPANS[1], lon % SPANS[2]

    planes = [plane * (SPANS[1] * SPANS[2]), (1 - plane) * (SPANS[1] * SPANS[2])]
    lines = [lax.rem(line + step, SPANS[1]) * SPANS[2] for step in range(SPANS[1])]
    places = [lax.rem(column_place + step, SPANS[2]) for step in range(SPANS[2])]

    def shifted(dz, dy, dx):
        return planes[dz] + lines[dy] + places[dx]

    for step in range(SPANS[1] - 1):
        greet((lat, shifted(0, far_first(step, SPANS[1]), 0)))
    for step in range(lats - 1):
        greet((lax.rem(lat + far_first(step, lats), lats), lon))
    for place in ((north, west), (north, east), (south, west), (south, east)):
        greet(place)
    greet((lat, west))
    greet((lat, east))
    greet((lat, shifted(1, 0, 0)))
    for step in range(1, SPANS[2]):
        greet((lat, shifted(0, 0, step)))

    loads[0].wait()
    edge_first[...] = field[:, :4]
    edge_last[...] = field[:, cols - 4 :]
    pl.semaphore_wait(barrier, lats - 1 + 4 + 2 + sum(SPANS) - len(SPANS))

    tail, head = pl.ds(rows - REACH, REACH), pl.ds(0, REACH)
    after, inner = pl.ds(rows + REACH, REACH), pl.ds(REACH, rows)
    halos = []
    for index, (source, target, place) in enumerate(
        (
            (edge_last, left.at[inner], (lat, east)),
            (edge_first, right.at[inner], (lat, west)),
            (field.at[tail], top, (south, lon)),
            (field.at[head], bottom, (north, lon)),
            (edge_last.at[tail], left.at[head], (south, east)),
            (edge_last.at[head], left.at[after], (north, east)),
            (edge_first.at[tail], right.at[head], (south, west)),
            (edge_first.at[head], right.at[after], (north, west)),
        )
    ):
        copy = pltpu.make_async_remote_copy(
            src_ref=source,
            dst_ref=target,
            send_sem=halo_send.at[index],
            recv_sem=halo_recv.at[index],
            device_id=place,
            device_id_type=MESH,
        )
        copy.start()
        halos.append(copy)

    def ready(index, place):
        pl.semaphore_signal(
            ready_sems.at[index], inc=1, device_id=place, device_id_type=MESH
        )

    for step in range(1, SPANS[2]):
        ready(0, (lat, shifted(0, 0, step)))

    def copy_to(phase, source, slot, place):
        return pltpu.make_async_remote_copy(
            src_ref=source,
            dst_ref=slot,
            send_sem=group_send.at[phase],
            recv_sem=group_recv.at[phase],
            device_id=place,
            device_id_type=MESH,
        )

    def all_of(phase, target, members):
        others = target.at[pl.ds(0, members - 1)]
        return copy_to(phase, others, others, (lat, lon))

    def exchange_lat(phase, source, target):
        for step in range(lats - 1):
            other = lax.rem(lat + far_first(step, lats), lats)
            copy_to(phase, source.at[other], target.at[lat], (other, lon)).start()
        target[lat] = source[lat]
        return all_of(phase, target, lats)

    loads[1].wait()
    taps_wide[...] = taps[...].astype(jnp.float32)
    padded[pl.ds(REACH, rows), :8] = jnp.zeros((rows, 8, channels), jnp.float32)
    padded[pl.ds(REACH, rows), 8 : 8 + cols] = wide(field)
    padded[pl.ds(REACH, rows), 8 + cols :] = jnp.zeros((rows, 8, channels), jnp.float32)
    sides[...] = jnp.zeros(sides.shape, jnp.float32)

    width = 2 * REACH + 1

    def tap_at(row_off, col_off, lanes):
        return taps_wide[row_off, col_off : col_off + 1, lanes]

    def add(sums, index, term):
        sums[index] = term if sums[index] is None else sums[index] + term

    def add_own(sums, view, col_off, lanes):
        for to_row in range(rows):
            for from_row in range(rows):
                row_off = from_row - to_row + REACH
                if 0 <= row_off < width:
                    add(sums, to_row, view[from_row] * tap_at(row_off, col_off, lanes))

    for half in range(channels // TILE):
        lanes = pl.ds(half * TILE, TILE)
        sums = [None] * rows
        for col_off in range(width):
            start = 8 - REACH + col_off
            add_own(sums, padded[pl.ds(REACH, rows), start : start + cols, lanes], col_off, lanes)
        for to_row in range(rows):
            convolved[to_row * cols : (to_row + 1) * cols, lanes] = sums[to_row]

    into, out_of = iotas((cells, cells))
    to_lon = (into // rows == out_of % cols) & (into % rows == out_of // cols)
    lon_packed = into // (rows * PACK) * PACK + into % PACK
    lat_packed = into // PACK % rows
    pack = out_of == lat_packed * cols + lon_packed
    pack_lon = out_of == lon_packed * rows + lat_packed
    lon_unpacked = out_of // (rows * PACK) * PACK + out_of % PACK
    unpack = into == (out_of // PACK % rows) * cols + lon_unpacked
    for index, chosen in enumerate((to_lon, pack, pack_lon, unpack)):
        orders[index] = chosen.astype(jnp.float32).astype(jnp.bfloat16)
    loads[2].wait()
    loads[3].wait()
    loads[4].wait()
    loads[5].wait()

    for copy in halos:
        copy.wait_recv()
    pl.semaphore_wait(ready_sems.at[0], SPANS[2] - 1)
    ready(1, (lat, shifted(1, 0, 0)))
    not_first = (lat > 0).astype(jnp.float32)
    not_last = (lat < lats - 1).astype(jnp.float32)
    padded[pl.ds(0, REACH), 8 : 8 + cols] = wide(top) * not_first
    padded[pl.ds(rows + REACH, REACH), 8 : 8 + cols] = wide(bottom) * not_last
    for side, start in ((left, 4), (right, 8 + cols)):
        values = wide(side)
        padded[pl.ds(0, REACH), start : start + 4] = values[:REACH] * not_first
        sides[:, start : start + 4] = values[REACH : REACH + rows]
        padded[pl.ds(rows + REACH, REACH), start : start + 4] = values[REACH + rows :] * not_last

    for half in range(channels // TILE):
        lanes = pl.ds(half * TILE, TILE)
        sums = [convolved[row * cols : (row + 1) * cols, lanes] for row in range(rows)]
        for col_off in range(width):
            start = 8 - REACH + col_off
            before = padded[pl.ds(0, REACH), start : start + cols, lanes]
            behind = padded[pl.ds(rows + REACH, REACH), start : start + cols, lanes]
            for from_row in range(REACH):
                for to_row in range(from_row + 1):
                    tap = tap_at(from_row - to_row, col_off, lanes)
                    add(sums, to_row, before[from_row] * tap)
                for to_row in range(rows - REACH + from_row, rows):
                    tap = tap_at(rows + REACH + from_row - to_row, col_off, lanes)
                    add(sums, to_row, behind[from_row] * tap)
        ends = []
        for first, offsets in ((0, range(REACH)), (cols - 8, range(REACH + 1, width))):
            strips = [None] * rows
            for col_off in offsets:
                start = 8 - REACH + col_off + first
                add_own(strips, sides[:, start : start + 8, lanes], col_off, lanes)
            ends.append(strips)
        for to_row in range(rows):
            strip = jnp.concatenate([ends[0][to_row], ends[1][to_row]], axis=0)
            convolved[to_row * cols : (to_row + 1) * cols, lanes] = sums[to_row] + strip

    normed = layer_norm(convolved[...]).astype(jnp.bfloat16)
    hidden = dot(normed, expand[...])
    hidden = 0.5 * hidden * (1.0 + lax.erf(hidden * (0.5**0.5)))
    own = field[...].astype(jnp.float32).reshape(cells, channels)
    block_one = (own + dot(hidden.astype(jnp.bfloat16), reduce[...])).astype(jnp.bfloat16)
    lat_in = layer_norm(block_one.astype(jnp.float32)).astype(jnp.bfloat16)

    by_lon = dot(orders[0], lat_in).astype(jnp.bfloat16)
    block_rows = cells // lats
    lat_out[...] = by_lon.reshape(lats, block_rows, channels)
    pending = exchange_lat(0, lat_out, lat_rows)
    block_packed[...] = dot(orders[1], block_one)
    pending.wait_recv()

    column = lat_rows[...].reshape(cells, channels)
    scale = head_size ** (-0.5) * math.log2(math.e)
    queries = (dot(column, lat_attn[0]) * scale).astype(jnp.bfloat16)
    keys = dot(column, lat_attn[1]).astype(jnp.bfloat16)
    values = dot(column, lat_attn[2]).astype(jnp.bfloat16)
    lane = lax.broadcasted_iota(jnp.int32, (cells, channels), 1)
    query_row, key_row = iotas((cells, cells))
    same = query_row // rows % (block_rows // rows) == key_row // rows % (block_rows // rows)

    def by_head(array):
        zeros = jnp.zeros_like(array)
        return jnp.concatenate(
            [jnp.where(lane // head_size == index, array, zeros) for index in range(HEADS)], axis=0
        )

    all_scores = dot_t(queries, by_head(keys))
    all_probs = []
    for head_index in range(HEADS):
        scores = all_scores[:, head_index * cells : (head_index + 1) * cells]
        scores = jnp.where(same, scores, -3e38)
        probs = jnp.exp2(scores - jnp.max(scores, axis=-1, keepdims=True))
        probs = probs * (1.0 / jnp.sum(probs, axis=-1, keepdims=True))
        all_probs.append(probs.astype(jnp.bfloat16))
    mixed = dot(jnp.concatenate(all_probs, axis=1), by_head(values))
    lat_mix_out[...] = mixed.astype(jnp.bfloat16).reshape(lats, block_rows, channels)
    pending.wait_send()
    pending = exchange_lat(1, lat_mix_out, lat_mix_rows)
    pending.wait_recv()

    lat_mix = dot(orders[2], lat_mix_rows[...].reshape(cells, channels)).astype(jnp.bfloat16)
    block_two = (block_packed[...] + dot(lat_mix, lat_attn[3])).astype(jnp.bfloat16)
    block_packed[...] = block_two.astype(jnp.float32)
    lon_in = layer_norm(block_two.astype(jnp.float32)).astype(jnp.bfloat16)
    part = rows * PACK
    spot = lax.broadcasted_iota(jnp.int32, (part, TILE), 1) // head_size
    for kind in range(3):
        projected = dot(lon_in, lon_attn[kind])
        if kind == 0:
            projected = projected * scale
        projected = projected.astype(jnp.bfloat16)
        for head_index in range(HEADS):
            tile, spot_from = head_index // per_tile * TILE, head_index % per_tile
            block = None
            for spot_to in range(per_tile):
                piece = projected[spot_to * part : (spot_to + 1) * part, tile : tile + TILE]
                if spot_to != spot_from:
                    piece = pltpu.roll(piece, (spot_to - spot_from) * head_size % TILE, 1)
                block = piece if block is None else jnp.where(spot == spot_to, piece, block)
            for row_index in range(rows):
                lon_out[row_index * HEADS + head_index, kind] = block[
                    row_index * PACK : (row_index + 1) * PACK
                ]
    pending.wait_send()
    pl.semaphore_wait(ready_sems.at[1], 1)

    for step in range(lons - 1):
        other = shifted(
            1 - step % 2,
            far_first(step // (SPANS[0] * SPANS[2]), SPANS[1]),
            far_first(step // SPANS[0] % SPANS[2], SPANS[2]),
        )
        copy_to(2, lon_out.at[other], lon_rows.at[lon], (lat, other)).start()
    lon_rows[lon] = lon_out[lon]
    pending = all_of(2, lon_rows, lons)
    source, target = iotas((TILE, per_tile * TILE))
    spread = target % TILE < head_size
    spread = spread & (source == target // TILE * head_size + target % TILE)
    spreading[...] = spread.astype(jnp.float32).astype(jnp.bfloat16)
    pending.wait_recv()

    length = lons * cols
    packed_rows = length // per_tile

    def apart(packed):
        return dot(packed, spreading[...]).astype(jnp.bfloat16)

    def stacked(parts):
        return jnp.concatenate(
            [parts[:, index * TILE : (index + 1) * TILE] for index in range(per_tile)], axis=0
        )

    keys = stacked(apart(lon_rows[:, 1].reshape(packed_rows, TILE)))
    values = stacked(apart(lon_rows[:, 2].reshape(packed_rows, TILE)))
    values = jnp.concatenate([values, jnp.ones((length, TILE), jnp.bfloat16)], axis=1)
    pending.wait_send()
    spread_queries = apart(lon_rows[:, 0].reshape(packed_rows, TILE))
    for index in range(per_tile):
        lon_queries[index] = spread_queries[:, index * TILE : (index + 1) * TILE]
    per_step = 4
    run = SPANS[2] * PACK
    def prepare(step):
        offsets = [
            (dz, far_first(step + index, SPANS[1])) for index in range(per_step) for dz in (1, 0)
        ]
        firsts = [planes[dz] + lines[dy] for dz, dy in offsets]
        spots = [pl.ds(pl.multiple_of(first * PACK, run), run) for first in firsts]
        queries = jnp.concatenate(
            [lon_queries[index, rows_of] for index in range(per_tile) for rows_of in spots], axis=0
        )
        scores = dot_t(queries, keys)
        return scores, firsts, offsets

    upcoming = prepare(0)
    for step in range(0, SPANS[1], per_step):
        scores, firsts, offsets = upcoming
        if step + per_step < SPANS[1]:
            upcoming = prepare(step + per_step)
        probs = jnp.exp2(scores - jnp.max(scores, axis=-1, keepdims=True))
        mixed = dot(probs.astype(jnp.bfloat16), values)
        mixed = mixed[:, :TILE] / mixed[:, TILE:]
        chunk = run * len(offsets)
        block = mixed[:chunk]
        for index in range(1, per_tile):
            piece = mixed[index * chunk : (index + 1) * chunk]
            block = block + pltpu.roll(piece, index * head_size, 1)
        block = block.astype(jnp.bfloat16)
        for index, (first, (dz, dy)) in enumerate(zip(firsts, offsets)):
            lon_mix_out[pl.ds(first, SPANS[2])] = block[index * run : (index + 1) * run].reshape(
                SPANS[2], PACK, TILE
            )
        for dz, dy in offsets:
            for dx in (2, 1, 3, 0):
                if (dz, dy, dx) != (0, 0, 0):
                    other = shifted(dz, dy, dx)
                    copy_to(3, lon_mix_out.at[other], lon_mix_rows.at[lon], (lat, other)).start()
    lon_mix_rows[lon] = lon_mix_out[lon]
    pending = all_of(3, lon_mix_rows, lons)
    pending.wait_recv()

    result = block_packed[...]
    for tile in range(channels // TILE):
        heads = [
            jnp.concatenate(
                [
                    lon_mix_rows[row_index * HEADS + head_index]
                    for row_index in range(rows)
                ],
                axis=0,
            )
            for head_index in range(per_tile * tile, per_tile * (tile + 1))
        ]
        parts = []
        for spot_from in range(per_tile):
            block = None
            for spot_to in range(per_tile):
                piece = heads[spot_to]
                if spot_to != spot_from:
                    piece = pltpu.roll(piece, (spot_to - spot_from) * head_size % TILE, 1)
                block = piece if block is None else jnp.where(spot == spot_to, piece, block)
            parts.append(block)
        mixture = jnp.concatenate(parts, axis=0)
        result = result + dot(mixture, lon_attn[3, tile * TILE : (tile + 1) * TILE])
    result = result.astype(jnp.bfloat16)
    for index in range(cols // PACK):
        for row_index in range(rows):
            start = index * part + row_index * PACK
            out_ref[row_index, index * PACK : (index + 1) * PACK] = result[start : start + PACK]
    pending.wait_send()
    for copy in halos:
        copy.wait_send()


def shards(lats, lons, field, dw_weight, w_expand, w_reduce, lat_attn, lon_attn):
    rows, cols, channels = field.shape
    cells = rows * cols
    bf16, f32 = jnp.bfloat16, jnp.float32
    arguments = (field, dw_weight, w_expand, w_reduce, lat_attn, lon_attn)
    vmem = pltpu.VMEM
    edge = vmem((rows, 4, channels), bf16)
    strip = vmem((REACH, cols, channels), bf16)
    side = vmem((rows + 2 * REACH, 4, channels), bf16)
    column = vmem((lats, cells // lats, channels), bf16)
    mix = vmem((lons, PACK, TILE), bf16)
    return pl.pallas_call(
        functools.partial(kernel, lats, lons),
        out_shape=jax.ShapeDtypeStruct(field.shape, field.dtype),
        in_specs=[pl.BlockSpec(memory_space=pltpu.HBM)] * len(arguments),
        out_specs=pl.BlockSpec(memory_space=pltpu.VMEM),
        scratch_shapes=[
            *(vmem(argument.shape, argument.dtype) for argument in arguments),
            edge,
            edge,
            strip,
            strip,
            side,
            side,
            vmem((rows + 2 * REACH, cols + 16, channels), f32),
            vmem((rows, cols + 16, channels), f32),
            vmem(dw_weight.shape, f32),
            vmem((cells, channels), f32),
            vmem((4, cells, cells), bf16),
            vmem((cells, channels), f32),
            column,
            column,
            column,
            column,
            vmem((lons, 3, PACK, TILE), bf16),
            vmem((lons, 3, PACK, TILE), bf16),
            mix,
            mix,
            vmem((TILE * HEADS // channels, lons * PACK, TILE), bf16),
            vmem((TILE, TILE * (TILE * HEADS // channels)), bf16),
            pltpu.SemaphoreType.DMA((len(arguments),)),
            pltpu.SemaphoreType.DMA((8,)),
            pltpu.SemaphoreType.DMA((8,)),
            pltpu.SemaphoreType.DMA((4,)),
            pltpu.SemaphoreType.DMA((4,)),
            pltpu.SemaphoreType.REGULAR((2,)),
        ],
        compiler_params=pltpu.CompilerParams(
            collective_id=0, has_side_effects=True, vmem_limit_bytes=48 << 20
        ),
        name="block",
    )(*(pltpu.with_memory_space_constraint(argument, pltpu.HBM) for argument in arguments))


def solution(mesh):
    return jax.shard_map(
        functools.partial(shards, mesh.shape["lat"], mesh.shape["lon"]),
        mesh=mesh,
        in_specs=(P("lat", "lon", None), P(), P(), P(), P(), P()),
        out_specs=P("lat", "lon", None),
        check_vma=False,
    )
```

```python
import functools
import math

import jax
import jax.numpy as jnp
from jax import lax
from jax.experimental import pallas as pl
from jax.experimental.pallas import tpu as pltpu
from jax.sharding import PartitionSpec as P

HEADS = 8
EPSILON = 1e-06
REACH = 3
TILE = 128
PACK = 4
SPANS = (2, 8, 4)
MESH = pl.DeviceIdType.MESH


def layer_norm(values):
    average = jnp.mean(values, axis=-1, keepdims=True)
    centered = values - average
    variance = jnp.mean(centered * centered, axis=-1, keepdims=True)
    return centered * lax.rsqrt(variance + EPSILON)


def dot(left, right):
    return jnp.dot(left, right, preferred_element_type=jnp.float32)


def dot_t(left, right):
    return lax.dot_general(left, right, (((1,), (1,)), ((), ())), preferred_element_type=jnp.float32)


def iotas(shape):
    return (lax.broadcasted_iota(jnp.int32, shape, 0), lax.broadcasted_iota(jnp.int32, shape, 1))


def far_first(step, members):
    return members // 2 + (step + 1) // 2 * (1 - 2 * (step % 2))


def wide(ref):
    return ref[...].astype(jnp.float32)


def kernel(
    lats,
    lons,
    field_hbm,
    taps_hbm,
    expand_hbm,
    reduce_hbm,
    lat_attn_hbm,
    lon_attn_hbm,
    out_ref,
    field,
    taps,
    expand,
    reduce,
    lat_attn,
    lon_attn,
    edge_first,
    edge_last,
    top,
    bottom,
    left,
    right,
    padded,
    sides,
    taps_wide,
    convolved,
    orders,
    block_packed,
    lat_out,
    lat_rows,
    lat_mix_out,
    lat_mix_rows,
    lon_out,
    lon_rows,
    lon_mix_out,
    lon_mix_rows,
    lon_queries,
    spreading,
    lon_values,
    load_sems,
    halo_send,
    halo_recv,
    group_send,
    group_recv,
    ready_sems,
):
    rows, cols, channels = field.shape
    cells = rows * cols
    head_size = channels // HEADS
    per_tile = TILE // head_size
    lat, lon = lax.axis_index("lat"), lax.axis_index("lon")

    loads = [
        pltpu.make_async_copy(source, target, load_sems.at[index])
        for index, (source, target) in enumerate(
            (
                (field_hbm, field),
                (taps_hbm, taps),
                (lon_attn_hbm, lon_attn),
                (expand_hbm, expand),
                (reduce_hbm, reduce),
                (lat_attn_hbm, lat_attn),
            )
        )
    ]
    for load in loads:
        load.start()

    north, south = lax.rem(lat + lats - 1, lats), lax.rem(lat + 1, lats)
    west, east = lax.rem(lon + lons - 1, lons), lax.rem(lon + 1, lons)

    barrier = pltpu.get_barrier_semaphore()

    def greet(place):
        pl.semaphore_signal(barrier, inc=1, device_id=place, device_id_type=MESH)

    plane, line, column_place = lon // (SPANS[1] * SPANS[2]), lon // SPANS[2] % SPANS[1], lon % SPANS[2]

    planes = [plane * (SPANS[1] * SPANS[2]), (1 - plane) * (SPANS[1] * SPANS[2])]
    lines = [lax.rem(line + step, SPANS[1]) * SPANS[2] for step in range(SPANS[1])]
    places = [lax.rem(column_place + step, SPANS[2]) for step in range(SPANS[2])]

    def shifted(dz, dy, dx):
        return planes[dz] + lines[dy] + places[dx]

    for step in range(SPANS[1] - 1):
        greet((lat, shifted(0, far_first(step, SPANS[1]), 0)))
    for step in range(lats - 1):
        greet((lax.rem(lat + far_first(step, lats), lats), lon))
    for place in ((north, west), (north, east), (south, west), (south, east)):
        greet(place)
    greet((lat, west))
    greet((lat, east))
    greet((lat, shifted(1, 0, 0)))
    for step in range(1, SPANS[2]):
        greet((lat, shifted(0, 0, step)))

    loads[0].wait()
    edge_first[...] = field[:, :4]
    edge_last[...] = field[:, cols - 4 :]
    pl.semaphore_wait(barrier, lats - 1 + 4 + 2 + sum(SPANS) - len(SPANS))

    tail, head = pl.ds(rows - REACH, REACH), pl.ds(0, REACH)
    after, inner = pl.ds(rows + REACH, REACH), pl.ds(REACH, rows)
    halos = []
    for index, (source, target, place) in enumerate(
        (
            (edge_last, left.at[inner], (lat, east)),
            (edge_first, right.at[inner], (lat, west)),
            (field.at[tail], top, (south, lon)),
            (field.at[head], bottom, (north, lon)),
            (edge_last.at[tail], left.at[head], (south, east)),
            (edge_last.at[head], left.at[after], (north, east)),
            (edge_first.at[tail], right.at[head], (south, west)),
            (edge_first.at[head], right.at[after], (north, west)),
        )
    ):
        copy = pltpu.make_async_remote_copy(
            src_ref=source,
            dst_ref=target,
            send_sem=halo_send.at[index],
            recv_sem=halo_recv.at[index],
            device_id=place,
            device_id_type=MESH,
        )
        copy.start()
        halos.append(copy)

    def ready(index, place):
        pl.semaphore_signal(
            ready_sems.at[index], inc=1, device_id=place, device_id_type=MESH
        )

    for step in range(1, SPANS[2]):
        ready(0, (lat, shifted(0, 0, step)))

    def copy_to(phase, source, slot, place):
        return pltpu.make_async_remote_copy(
            src_ref=source,
            dst_ref=slot,
            send_sem=group_send.at[phase],
            recv_sem=group_recv.at[phase],
            device_id=place,
            device_id_type=MESH,
        )

    def all_of(phase, target, members):
        others = target.at[pl.ds(0, members - 1)]
        return copy_to(phase, others, others, (lat, lon))

    def exchange_lat(phase, source, target):
        for step in range(lats - 1):
            other = lax.rem(lat + far_first(step, lats), lats)
            copy_to(phase, source.at[other], target.at[lat], (other, lon)).start()
        target[lat] = source[lat]
        return all_of(phase, target, lats)

    loads[1].wait()
    taps_wide[...] = taps[...].astype(jnp.float32)
    padded[pl.ds(REACH, rows), :8] = jnp.zeros((rows, 8, channels), jnp.float32)
    padded[pl.ds(REACH, rows), 8 : 8 + cols] = wide(field)
    padded[pl.ds(REACH, rows), 8 + cols :] = jnp.zeros((rows, 8, channels), jnp.float32)
    sides[...] = jnp.zeros(sides.shape, jnp.float32)

    width = 2 * REACH + 1

    def tap_at(row_off, col_off, lanes):
        return taps_wide[row_off, col_off : col_off + 1, lanes]

    def add(sums, index, term):
        sums[index] = term if sums[index] is None else sums[index] + term

    def add_own(sums, view, col_off, lanes):
        for to_row in range(rows):
            for from_row in range(rows):
                row_off = from_row - to_row + REACH
                if 0 <= row_off < width:
                    add(sums, to_row, view[from_row] * tap_at(row_off, col_off, lanes))

    for half in range(channels // TILE):
        lanes = pl.ds(half * TILE, TILE)
        sums = [None] * rows
        for col_off in range(width):
            start = 8 - REACH + col_off
            add_own(sums, padded[pl.ds(REACH, rows), start : start + cols, lanes], col_off, lanes)
        for to_row in range(rows):
            convolved[to_row * cols : (to_row + 1) * cols, lanes] = sums[to_row]

    into, out_of = iotas((cells, cells))
    to_lon = (into // rows == out_of % cols) & (into % rows == out_of // cols)
    lon_packed = into // (rows * PACK) * PACK + into % PACK
    lat_packed = into // PACK % rows
    pack = out_of == lat_packed * cols + lon_packed
    pack_lon = out_of == lon_packed * rows + lat_packed
    lon_unpacked = out_of // (rows * PACK) * PACK + out_of % PACK
    unpack = into == (out_of // PACK % rows) * cols + lon_unpacked
    for index, chosen in enumerate((to_lon, pack, pack_lon, unpack)):
        orders[index] = chosen.astype(jnp.float32).astype(jnp.bfloat16)
    loads[2].wait()
    loads[3].wait()
    loads[4].wait()
    loads[5].wait()

    for copy in halos:
        copy.wait_recv()
    pl.semaphore_wait(ready_sems.at[0], SPANS[2] - 1)
    ready(1, (lat, shifted(1, 0, 0)))
    not_first = (lat > 0).astype(jnp.float32)
    not_last = (lat < lats - 1).astype(jnp.float32)
    padded[pl.ds(0, REACH), 8 : 8 + cols] = wide(top) * not_first
    padded[pl.ds(rows + REACH, REACH), 8 : 8 + cols] = wide(bottom) * not_last
    for side, start in ((left, 4), (right, 8 + cols)):
        values = wide(side)
        padded[pl.ds(0, REACH), start : start + 4] = values[:REACH] * not_first
        sides[:, start : start + 4] = values[REACH : REACH + rows]
        padded[pl.ds(rows + REACH, REACH), start : start + 4] = values[REACH + rows :] * not_last

    for half in range(channels // TILE):
        lanes = pl.ds(half * TILE, TILE)
        sums = [convolved[row * cols : (row + 1) * cols, lanes] for row in range(rows)]
        for col_off in range(width):
            start = 8 - REACH + col_off
            before = padded[pl.ds(0, REACH), start : start + cols, lanes]
            behind = padded[pl.ds(rows + REACH, REACH), start : start + cols, lanes]
            for from_row in range(REACH):
                for to_row in range(from_row + 1):
                    tap = tap_at(from_row - to_row, col_off, lanes)
                    add(sums, to_row, before[from_row] * tap)
                for to_row in range(rows - REACH + from_row, rows):
                    tap = tap_at(rows + REACH + from_row - to_row, col_off, lanes)
                    add(sums, to_row, behind[from_row] * tap)
        ends = []
        for first, offsets in ((0, range(REACH)), (cols - 8, range(REACH + 1, width))):
            strips = [None] * rows
            for col_off in offsets:
                start = 8 - REACH + col_off + first
                add_own(strips, sides[:, start : start + 8, lanes], col_off, lanes)
            ends.append(strips)
        for to_row in range(rows):
            strip = jnp.concatenate([ends[0][to_row], ends[1][to_row]], axis=0)
            convolved[to_row * cols : (to_row + 1) * cols, lanes] = sums[to_row] + strip

    normed = layer_norm(convolved[...]).astype(jnp.bfloat16)
    hidden = dot(normed, expand[...])
    hidden = 0.5 * hidden * (1.0 + lax.erf(hidden * (0.5**0.5)))
    own = field[...].astype(jnp.float32).reshape(cells, channels)
    block_one = (own + dot(hidden.astype(jnp.bfloat16), reduce[...])).astype(jnp.bfloat16)
    lat_in = layer_norm(block_one.astype(jnp.float32)).astype(jnp.bfloat16)

    by_lon = dot(orders[0], lat_in).astype(jnp.bfloat16)
    block_rows = cells // lats
    lat_out[...] = by_lon.reshape(lats, block_rows, channels)
    pending = exchange_lat(0, lat_out, lat_rows)
    block_packed[...] = dot(orders[1], block_one)
    pending.wait_recv()

    column = lat_rows[...].reshape(cells, channels)
    scale = head_size ** (-0.5) * math.log2(math.e)
    queries = (dot(column, lat_attn[0]) * scale).astype(jnp.bfloat16)
    keys = dot(column, lat_attn[1]).astype(jnp.bfloat16)
    values = dot(column, lat_attn[2]).astype(jnp.bfloat16)
    lane = lax.broadcasted_iota(jnp.int32, (cells, channels), 1)
    query_row, key_row = iotas((cells, cells))
    same = query_row // rows % (block_rows // rows) == key_row // rows % (block_rows // rows)

    def by_head(array):
        zeros = jnp.zeros_like(array)
        return jnp.concatenate(
            [jnp.where(lane // head_size == index, array, zeros) for index in range(HEADS)], axis=0
        )

    all_scores = dot_t(queries, by_head(keys))
    all_probs = []
    for head_index in range(HEADS):
        scores = all_scores[:, head_index * cells : (head_index + 1) * cells]
        scores = jnp.where(same, scores, -3e38)
        probs = jnp.exp2(scores - jnp.max(scores, axis=-1, keepdims=True))
        probs = probs * (1.0 / jnp.sum(probs, axis=-1, keepdims=True))
        all_probs.append(probs.astype(jnp.bfloat16))
    mixed = dot(jnp.concatenate(all_probs, axis=1), by_head(values))
    lat_mix_out[...] = mixed.astype(jnp.bfloat16).reshape(lats, block_rows, channels)
    pending.wait_send()
    pending = exchange_lat(1, lat_mix_out, lat_mix_rows)
    pending.wait_recv()

    lat_mix = dot(orders[2], lat_mix_rows[...].reshape(cells, channels)).astype(jnp.bfloat16)
    block_two = (block_packed[...] + dot(lat_mix, lat_attn[3])).astype(jnp.bfloat16)
    block_packed[...] = block_two.astype(jnp.float32)
    lon_in = layer_norm(block_two.astype(jnp.float32)).astype(jnp.bfloat16)
    part = rows * PACK
    spot = lax.broadcasted_iota(jnp.int32, (part, TILE), 1) // head_size
    for kind in range(3):
        projected = dot(lon_in, lon_attn[kind])
        if kind == 0:
            projected = projected * scale
        projected = projected.astype(jnp.bfloat16)
        for head_index in range(HEADS):
            tile, spot_from = head_index // per_tile * TILE, head_index % per_tile
            block = None
            for spot_to in range(per_tile):
                piece = projected[spot_to * part : (spot_to + 1) * part, tile : tile + TILE]
                if spot_to != spot_from:
                    piece = pltpu.roll(piece, (spot_to - spot_from) * head_size % TILE, 1)
                block = piece if block is None else jnp.where(spot == spot_to, piece, block)
            for row_index in range(rows):
                lon_out[row_index * HEADS + head_index, kind] = block[
                    row_index * PACK : (row_index + 1) * PACK
                ]
    pending.wait_send()
    pl.semaphore_wait(ready_sems.at[1], 1)

    for step in range(lons - 1):
        other = shifted(
            1 - step % 2,
            far_first(step // (SPANS[0] * SPANS[2]), SPANS[1]),
            far_first(step // SPANS[0] % SPANS[2], SPANS[2]),
        )
        copy_to(2, lon_out.at[other], lon_rows.at[lon], (lat, other)).start()
    lon_rows[lon] = lon_out[lon]
    pending = all_of(2, lon_rows, lons)
    lon_values[:, TILE:] = jnp.ones((lons * cols, TILE), jnp.bfloat16)
    source, target = iotas((TILE, per_tile * TILE))
    spread = target % TILE < head_size
    spread = spread & (source == target // TILE * head_size + target % TILE)
    spreading[...] = spread.astype(jnp.float32).astype(jnp.bfloat16)
    pending.wait_recv()

    length = lons * cols
    packed_rows = length // per_tile

    def apart(packed):
        return dot(packed, spreading[...]).astype(jnp.bfloat16)

    def stacked(parts):
        return jnp.concatenate(
            [parts[:, index * TILE : (index + 1) * TILE] for index in range(per_tile)], axis=0
        )

    keys = stacked(apart(lon_rows[:, 1].reshape(packed_rows, TILE)))
    lon_values[:, :TILE] = stacked(apart(lon_rows[:, 2].reshape(packed_rows, TILE)))
    pending.wait_send()
    spread_queries = apart(lon_rows[:, 0].reshape(packed_rows, TILE))
    for index in range(per_tile):
        lon_queries[index] = spread_queries[:, index * TILE : (index + 1) * TILE]
    per_step = 4
    run = SPANS[2] * PACK
    def prepare(step):
        offsets = [
            (dz, far_first(step + index, SPANS[1])) for index in range(per_step) for dz in (1, 0)
        ]
        firsts = [planes[dz] + lines[dy] for dz, dy in offsets]
        spots = [pl.ds(pl.multiple_of(first * PACK, run), run) for first in firsts]
        queries = jnp.concatenate(
            [lon_queries[index, rows_of] for index in range(per_tile) for rows_of in spots], axis=0
        )
        scores = dot_t(queries, keys)
        return scores, firsts, offsets

    upcoming = prepare(0)
    for step in range(0, SPANS[1], per_step):
        scores, firsts, offsets = upcoming
        if step + per_step < SPANS[1]:
            upcoming = prepare(step + per_step)
        probs = jnp.exp2(scores - jnp.max(scores, axis=-1, keepdims=True))
        mixed = dot(probs.astype(jnp.bfloat16), lon_values[...])
        mixed = mixed[:, :TILE] / mixed[:, TILE:]
        chunk = run * len(offsets)
        block = mixed[:chunk]
        for index in range(1, per_tile):
            piece = mixed[index * chunk : (index + 1) * chunk]
            block = block + pltpu.roll(piece, index * head_size, 1)
        block = block.astype(jnp.bfloat16)
        for index, (first, (dz, dy)) in enumerate(zip(firsts, offsets)):
            lon_mix_out[pl.ds(first, SPANS[2])] = block[index * run : (index + 1) * run].reshape(
                SPANS[2], PACK, TILE
            )
        for dz, dy in offsets:
            for dx in (2, 1, 3, 0):
                if (dz, dy, dx) != (0, 0, 0):
                    other = shifted(dz, dy, dx)
                    copy_to(3, lon_mix_out.at[other], lon_mix_rows.at[lon], (lat, other)).start()
    lon_mix_rows[lon] = lon_mix_out[lon]
    pending = all_of(3, lon_mix_rows, lons)
    pending.wait_recv()

    result = block_packed[...]
    for tile in range(channels // TILE):
        heads = [
            jnp.concatenate(
                [
                    lon_mix_rows[row_index * HEADS + head_index]
                    for row_index in range(rows)
                ],
                axis=0,
            )
            for head_index in range(per_tile * tile, per_tile * (tile + 1))
        ]
        parts = []
        for spot_from in range(per_tile):
            block = None
            for spot_to in range(per_tile):
                piece = heads[spot_to]
                if spot_to != spot_from:
                    piece = pltpu.roll(piece, (spot_to - spot_from) * head_size % TILE, 1)
                block = piece if block is None else jnp.where(spot == spot_to, piece, block)
            parts.append(block)
        mixture = jnp.concatenate(parts, axis=0)
        result = result + dot(mixture, lon_attn[3, tile * TILE : (tile + 1) * TILE])
    result = result.astype(jnp.bfloat16)
    for index in range(cols // PACK):
        for row_index in range(rows):
            start = index * part + row_index * PACK
            out_ref[row_index, index * PACK : (index + 1) * PACK] = result[start : start + PACK]
    pending.wait_send()
    for copy in halos:
        copy.wait_send()


def shards(lats, lons, field, dw_weight, w_expand, w_reduce, lat_attn, lon_attn):
    rows, cols, channels = field.shape
    cells = rows * cols
    bf16, f32 = jnp.bfloat16, jnp.float32
    arguments = (field, dw_weight, w_expand, w_reduce, lat_attn, lon_attn)
    vmem = pltpu.VMEM
    edge = vmem((rows, 4, channels), bf16)
    strip = vmem((REACH, cols, channels), bf16)
    side = vmem((rows + 2 * REACH, 4, channels), bf16)
    column = vmem((lats, cells // lats, channels), bf16)
    mix = vmem((lons, PACK, TILE), bf16)
    return pl.pallas_call(
        functools.partial(kernel, lats, lons),
        out_shape=jax.ShapeDtypeStruct(field.shape, field.dtype),
        in_specs=[pl.BlockSpec(memory_space=pltpu.HBM)] * len(arguments),
        out_specs=pl.BlockSpec(memory_space=pltpu.VMEM),
        scratch_shapes=[
            *(vmem(argument.shape, argument.dtype) for argument in arguments),
            edge,
            edge,
            strip,
            strip,
            side,
            side,
            vmem((rows + 2 * REACH, cols + 16, channels), f32),
            vmem((rows, cols + 16, channels), f32),
            vmem(dw_weight.shape, f32),
            vmem((cells, channels), f32),
            vmem((4, cells, cells), bf16),
            vmem((cells, channels), f32),
            column,
            column,
            column,
            column,
            vmem((lons, 3, PACK, TILE), bf16),
            vmem((lons, 3, PACK, TILE), bf16),
            mix,
            mix,
            vmem((TILE * HEADS // channels, lons * PACK, TILE), bf16),
            vmem((TILE, TILE * (TILE * HEADS // channels)), bf16),
            vmem((lons * cols, 2 * TILE), bf16),
            pltpu.SemaphoreType.DMA((len(arguments),)),
            pltpu.SemaphoreType.DMA((8,)),
            pltpu.SemaphoreType.DMA((8,)),
            pltpu.SemaphoreType.DMA((4,)),
            pltpu.SemaphoreType.DMA((4,)),
            pltpu.SemaphoreType.REGULAR((2,)),
        ],
        compiler_params=pltpu.CompilerParams(
            collective_id=0, has_side_effects=True, vmem_limit_bytes=48 << 20
        ),
        name="block",
    )(*(pltpu.with_memory_space_constraint(argument, pltpu.HBM) for argument in arguments))


def solution(mesh):
    return jax.shard_map(
        functools.partial(shards, mesh.shape["lat"], mesh.shape["lon"]),
        mesh=mesh,
        in_specs=(P("lat", "lon", None), P(), P(), P(), P(), P()),
        out_specs=P("lat", "lon", None),
        check_vma=False,
    )
```
